32 devices in a mesh: groups: 2 (over x), win: 8 (over z, y), gx: 2 (over core).
Axes of the slice: x: 2, y: 2, z: 4, core: 2. Of those that a mesh axis runs over, the one named last changes fastest.
Arguments:
- prev_states: float32 [16, 1024, 128], P(('groups', 'win'), 'gx'), parts along dimension 0, may hold values from -6 to 6
- timesteps: int32 [16], P(('groups', 'win')), parts along dimension 0, may hold values from 0 to 999
- step_sizes: float32 [16], P(('groups', 'win')), parts along dimension 0, may hold values from 0.1 to 0.3
- slide: int32 [1], replicated, may hold values from 1 to 8
- w_time: bfloat16 [256, 768], replicated, may hold values from -0.375 to 0.375
- w_ada: bfloat16 [1, 768, 4608], replicated, may hold values from -0.21875 to 0.21875
- w_in: bfloat16 [128, 768], replicated, may hold values from -0.5 to 0.5
- w_qkv: bfloat16 [1, 768, 2304], replicated, may hold values from -2 to 2
- w_proj: bfloat16 [1, 768, 768], replicated, may hold values from -0.21875 to 0.21875
- w_up: bfloat16 [1, 768, 3072], replicated, may hold values from -0.21875 to 0.21875
- w_down: bfloat16 [1, 3072, 768], replicated, may hold values from -0.109375 to 0.109375
- w_out: bfloat16 [768, 128], replicated, may hold values from -0.21875 to 0.21875
Outputs:
- states_out: float32 [16, 1024, 128], P(('groups', 'win'), 'gx'), parts along dimension 0
The draws below stay inside these ranges and needn't reach their ends.
There are 2 independent parts, one for each index of `groups`. The reference program is written for one: setup_inputs(seed, part) draws one part's arguments, and reference() takes and returns one part's arrays. A program takes and returns all parts, laid end to end along the dimension named above; an argument that names none is the same for every part. Nothing has to cross between parts.
All inputs are finite; a program needn't handle non-finite values.
Results may differ from the reference program's by a relative error of at most 0.0043.
Values may be sent and summed in bfloat16 or wider, within the bound.
No kernel may reach another device: no remote copies, remote signals or barrier semaphores. Data moves between devices by JAX's collectives and lax.ppermute only.
A program may use at most 128 MiB of HBM per device.

```python
import math
import jax
import jax.numpy as jnp
from jax import lax

D = 768
HEADS = 12
FF = 3072
FREQ = 256
CHAN = 128
LAYERS = 1
SWEEPS = 2
GY = 8
GZ = 8
TOKENS = 1024
N_WIN = 8


def draw_w_qkv(key, part):
    base_key = jax.random.fold_in(jax.random.fold_in(key, 7), 0)
    weights = jax.random.normal(base_key, (LAYERS, D, 3 * D), jnp.float32) / jnp.sqrt(jnp.float32(D))
    return jnp.clip(weights, -2.0, 2.0).astype(jnp.bfloat16)


def set_ends(result, key, least, top_value):
    longest = result.shape.index(max(result.shape))
    spots = []
    for shift in (0, 1):
        where = [jax.random.randint(jax.random.fold_in(key, axis), (), 0, length) for axis, length in enumerate(result.shape)]
        where[longest] = (where[longest] + shift) % result.shape[longest]
        spots.append(tuple(where))
    return result.at[spots[0]].set(least).at[spots[1]].set(top_value)


def steps_of(rng, dims, shards, low, largest):
    loudness = 1.0
    for position, parts in shards:
        draws = jax.random.uniform(jax.random.fold_in(jax.random.fold_in(rng, 6), position), (parts,), jnp.float32, low / len(shards), largest / len(shards))
        loudness = loudness * jnp.repeat(jnp.exp(draws), dims[position] // parts).reshape((-1,) + (1,) * (len(dims) - 1 - position))
    return loudness


def bell_draw(key, extent, scale, most, cuts=(), kind=jnp.bfloat16):
    entries = scale * jax.random.normal(key, extent, jnp.float32)
    if cuts:
        entries = entries * steps_of(key, extent, cuts, -0.22, 0.18)
    return jnp.clip(entries, -most, most).astype(kind)


def setup_inputs(seed: int = 0, part: int = 0) -> dict:
    streams_of = jax.random.split(jax.random.key(seed), 13)
    own_keys = jax.random.split(jax.random.fold_in(streams_of[12], part), 13)
    prev_states = bell_draw(own_keys[0], (N_WIN, TOKENS, CHAN), 1.0, 6.0, ((0, 8), (1, 2)), jnp.float32)
    timesteps = set_ends(jax.random.randint(own_keys[1], (N_WIN,), 0, 1000), jax.random.fold_in(own_keys[1], 1), 0, 999).astype(jnp.int32)
    step_sizes = jnp.clip(jnp.exp(math.log(0.3) - 1.0986123 * jax.random.uniform(own_keys[2], (N_WIN,), jnp.float32) ** steps_of(own_keys[2], (N_WIN,), ((0, 8),), -0.2, 0.2)), 0.1, 0.3)
    slide = jax.random.randint(streams_of[3], (1,), 1, N_WIN + 1).astype(jnp.int32)
    w_time = bell_draw(streams_of[4], (FREQ, D), FREQ ** -0.5, 0.375)
    w_ada = bell_draw(streams_of[5], (LAYERS, D, 6 * D), D ** -0.5, 0.21875)
    w_in = bell_draw(streams_of[6], (CHAN, D), CHAN ** -0.5, 0.5)
    w_qkv = draw_w_qkv(jax.random.fold_in(streams_of[12], 71), part)
    w_proj = bell_draw(streams_of[8], (LAYERS, D, D), D ** -0.5, 0.21875)
    w_up = bell_draw(streams_of[9], (LAYERS, D, FF), D ** -0.5, 0.21875)
    w_down = bell_draw(streams_of[10], (LAYERS, FF, D), FF ** -0.5, 0.109375)
    w_out = bell_draw(streams_of[11], (D, CHAN), D ** -0.5, 0.21875)
    return {"prev_states": prev_states, "timesteps": timesteps, "step_sizes": step_sizes, "slide": slide, "w_time": w_time, "w_ada": w_ada, "w_in": w_in, "w_qkv": w_qkv, "w_proj": w_proj, "w_up": w_up, "w_down": w_down, "w_out": w_out}


EPSILON = 1e-06

def layer_norm(values):
    centred = values - lax.optimization_barrier(jnp.mean(values, axis=-1, keepdims=True))
    spread = lax.optimization_barrier(jnp.mean(centred * centred, axis=-1, keepdims=True))
    return centred * lax.rsqrt(spread + EPSILON)

def modulation(moment, w_time, w_ada):
    half = w_time.shape[0] // 2
    freqs = jnp.exp(-math.log(10000.0) * jnp.arange(half, dtype=jnp.float32) / half)
    angles = moment.astype(jnp.float32) * freqs
    embedded = jnp.concatenate([jnp.cos(angles), jnp.sin(angles)])[None, :]
    condition = jax.nn.silu(jnp.dot(embedded.astype(jnp.bfloat16), w_time, preferred_element_type=jnp.float32))
    active = jax.nn.silu(condition).astype(jnp.bfloat16)
    return jnp.stack([jnp.dot(active, w_ada[layer_index], preferred_element_type=jnp.float32).reshape(6, -1) for layer_index in range(w_ada.shape[0])])

def neighbour_mask():
    cells = jnp.arange(GY * GZ, dtype=jnp.int32)
    row_y = cells // GZ
    row_z = cells % GZ
    apart_y = (row_y[None, :] - row_y[:, None]) % GY
    apart_z = (row_z[None, :] - row_z[:, None]) % GZ
    near = (jnp.minimum(apart_y, GY - apart_y) <= 3) & (jnp.minimum(apart_z, GZ - apart_z) <= 3)
    return jnp.tile(near, (1, 7))

def attend(queries, keys, values, mask):
    planes, cells, width = queries.shape
    head_size = width // HEADS
    key_window = jnp.concatenate([keys[offset_plane:offset_plane + planes] for offset_plane in range(7)], axis=1)
    value_window = jnp.concatenate([values[offset_plane:offset_plane + planes] for offset_plane in range(7)], axis=1)
    query_heads = queries.reshape(planes, cells, HEADS, head_size).astype(jnp.float32)
    key_heads = key_window.reshape(planes, 7 * cells, HEADS, head_size).astype(jnp.float32)
    value_heads = value_window.reshape(planes, 7 * cells, HEADS, head_size).astype(jnp.float32)
    scores = jnp.einsum('pshe,pkhe->phsk', query_heads, key_heads) * head_size ** (-0.5)
    scores = jnp.where(mask, scores, -1e+30)
    peak = lax.optimization_barrier(jnp.max(scores, axis=-1, keepdims=True))
    raised = jnp.exp(scores - peak)
    weights = (raised / lax.optimization_barrier(jnp.sum(raised, axis=-1, keepdims=True))).astype(jnp.bfloat16)
    mixed = jnp.einsum('phsk,pkhe->pshe', weights.astype(jnp.float32), value_heads)
    return mixed.astype(jnp.bfloat16).reshape(planes, cells, width)

def block_layer(hidden, mods, w_qkv, w_proj, w_up, w_down, mask):
    planes, cells, width = hidden.shape
    normed = (layer_norm(hidden) * (1.0 + mods[1]) + mods[0]).astype(jnp.bfloat16)
    packed = jnp.dot(normed.reshape(-1, width), w_qkv, preferred_element_type=jnp.float32).astype(jnp.bfloat16)
    packed = packed.reshape(planes, cells, 3 * width)
    queries = packed[..., :width]
    keys = packed[..., width:2 * width]
    values = packed[..., 2 * width:]
    keys = jnp.concatenate([keys[-3:], keys, keys[:3]], axis=0)
    values = jnp.concatenate([values[-3:], values, values[:3]], axis=0)
    attended = attend(queries, keys, values, mask)
    hidden = hidden + mods[2] * jnp.dot(attended.reshape(-1, width), w_proj, preferred_element_type=jnp.float32).reshape(planes, cells, width)
    normed = (layer_norm(hidden) * (1.0 + mods[4]) + mods[3]).astype(jnp.bfloat16)
    inner = jax.nn.gelu(jnp.dot(normed.reshape(-1, width), w_up, preferred_element_type=jnp.float32), approximate=True).astype(jnp.bfloat16)
    return hidden + mods[5] * jnp.dot(inner, w_down, preferred_element_type=jnp.float32).reshape(planes, cells, width)

def field_drift(states_now, mod_rows, weights, mask):
    w_in, w_qkv, w_proj, w_up, w_down, w_out = weights
    cells = GY * GZ
    planes = states_now.shape[0] // cells
    hidden = jnp.dot(states_now.astype(jnp.bfloat16), w_in, preferred_element_type=jnp.float32).reshape(planes, cells, -1)
    for layer_index in range(w_qkv.shape[0]):
        hidden = block_layer(hidden, mod_rows[layer_index], w_qkv[layer_index], w_proj[layer_index], w_up[layer_index], w_down[layer_index], mask)
    width = hidden.shape[-1]
    return jnp.dot(layer_norm(hidden).astype(jnp.bfloat16).reshape(-1, width), w_out, preferred_element_type=jnp.float32)

def reference(prev_states, timesteps, step_sizes, slide, w_time, w_ada, w_in, w_qkv, w_proj, w_up, w_down, w_out):
    window = N_WIN
    offset = (slide[0] - 1).astype(jnp.int32)
    targets = jnp.minimum(jnp.arange(window, dtype=jnp.int32) + offset, window - 1).astype(jnp.int32)
    iterate = jnp.take(prev_states, targets, axis=0)
    start = lax.dynamic_index_in_dim(prev_states, offset, 0, keepdims=False)
    mask = neighbour_mask()
    weights = (w_in, w_qkv, w_proj, w_up, w_down, w_out)

    def one_drift(pair):
        states_now, moment = pair
        return field_drift(states_now, modulation(moment, w_time, w_ada), weights, mask)
    total = iterate
    for sweep_index in range(SWEEPS):
        drift = lax.map(one_drift, (iterate, timesteps))
        increment = step_sizes[:, None, None] * drift
        total = jnp.cumsum(increment, axis=0)
        iterate = start[None] + (total - increment)
    return start[None] + total
```

```python
import functools
import math

import jax
import jax.numpy as jnp
from jax import lax
from jax.experimental import pallas as pl
from jax.experimental.pallas import tpu as pltpu
from jax.sharding import PartitionSpec as P

HEADS = 12
SWEEPS = 2
GY = 8
GZ = 8
REACH = 3
EPSILON = 1e-06
FAR = -(2.0**100)
LANES = 128
F32 = jnp.float32
BF16 = jnp.bfloat16


def dot(a, b):
    return lax.dot_general(a, b, (((1,), (0,)), ((), ())), preferred_element_type=F32)


def dot_t(a, b):
    return lax.dot_general(a, b, (((1,), (1,)), ((), ())), preferred_element_type=F32)


def layer_norm(values):
    centred = values - jnp.mean(values, axis=-1, keepdims=True)
    spread = jnp.mean(centred * centred, axis=-1, keepdims=True)
    return centred * lax.rsqrt(spread + EPSILON)


def silu(x):
    return x / (1.0 + jnp.exp(-x))


def gelu(x):
    inner = x * (math.sqrt(2.0 / math.pi) + (math.sqrt(2.0 / math.pi) * 0.044715) * (x * x))
    half = 0.5 * x
    return half + half * jnp.tanh(inner)


def mods_kernel(emb_ref, w_time_ref, w_ada_ref, out_ref):
    condition = silu(dot(emb_ref[...], w_time_ref[...]))
    active = silu(condition).astype(BF16)
    out_ref[...] = dot(active, w_ada_ref[...])


def modulation(moment, w_time, w_ada):
    half = w_time.shape[0] // 2
    freqs = jnp.exp(-math.log(10000.0) * jnp.arange(half, dtype=F32) / half)
    angles = moment.astype(F32) * freqs
    embedded = jnp.concatenate([jnp.cos(angles), jnp.sin(angles)]).astype(BF16)
    embedded = jnp.broadcast_to(embedded[None], (8, embedded.shape[0]))
    depth, wide = w_ada.shape[1:]
    steps = 6
    out = pl.pallas_call(
        mods_kernel,
        grid=(steps,),
        in_specs=[
            pl.BlockSpec(embedded.shape, lambda i: (0, 0)),
            pl.BlockSpec(w_time.shape, lambda i: (0, 0)),
            pl.BlockSpec((depth, wide // steps), lambda i: (0, i)),
        ],
        out_specs=pl.BlockSpec((8, wide // steps), lambda i: (0, i)),
        out_shape=jax.ShapeDtypeStruct((8, wide), F32),
        compiler_params=pltpu.CompilerParams(vmem_limit_bytes=16 << 20),
        name="mods",
    )(embedded, w_time, w_ada[0])
    return out[0].reshape(6, -1)


def sweep_kernel(
    halo_right, halo_left,
    own_ref, halo_ref, mods_ref, step_ref,
    w_in_hbm, w_qkv_hbm, w_proj_hbm, w_up_hbm, w_down_hbm, w_out_hbm,
    inc_ref,
    w_in, w_qkv, w_proj, w_up, w_down, w_out,
    h_scr, a_scr, ah_scr, q_scr, k_scr, v_scr, o_scr, g_scr, qmask, kmask, sems,
):
    pairs = (
        (w_in_hbm, w_in), (w_qkv_hbm, w_qkv), (w_proj_hbm, w_proj),
        (w_up_hbm, w_up), (w_down_hbm, w_down), (w_out_hbm, w_out),
    )
    copies = [pltpu.make_async_copy(s, d, sems.at[i]) for i, (s, d) in enumerate(pairs)]
    for c in copies:
        c.start()
    rows, width = h_scr.shape
    rim = REACH * GY * GZ
    head = width // HEADS
    tile = 256
    shift1, scale1, gate1 = mods_ref[0:1, :], 1.0 + mods_ref[1:2, :], mods_ref[2:3, :]
    shift2, scale2, gate2 = mods_ref[3:4, :], 1.0 + mods_ref[4:5, :], mods_ref[5:6, :]

    r = lax.broadcasted_iota(jnp.int32, (LANES, LANES), 0)
    f = lax.broadcasted_iota(jnp.int32, (LANES, LANES), 1)
    cell = r % (GY * GZ)
    hit = (
        (f == cell // GZ) | (f == GY + cell % GZ) | (f == GY + GZ + r // (GY * GZ))
    )
    qmask[...] = jnp.where(hit, FAR, 0.0).astype(BF16)
    keys = kmask.shape[0]
    r = lax.broadcasted_iota(jnp.int32, (keys, LANES), 0)
    f = lax.broadcasted_iota(jnp.int32, (keys, LANES), 1)
    cell = r % (GY * GZ)
    plane = r // (GY * GZ)
    hit = (
        (f == (cell // GZ + GY // 2) % GY)
        | (f == GY + (cell % GZ + GZ // 2) % GZ)
        | ((f == GY + GZ) & (plane == 2 * REACH + 1))
        | ((f == GY + GZ + 1) & (plane == 0))
    )
    kmask[...] = jnp.where(hit, 1.0, 0.0).astype(BF16)

    copies[0].wait()

    def embed(x):
        h = dot(x, w_in[...])
        return h, (layer_norm(h) * scale1 + shift1).astype(BF16)

    part = 128

    @pl.loop(0, rows // part)
    def _(i):
        at = pl.ds(pl.multiple_of(i * part, part), part)
        h, a = embed(own_ref[at, :])
        h_scr[at, :] = h
        a_scr[at, :] = a

    ah_scr[0:rim, :] = embed(halo_ref[halo_left:halo_left + rim, :])[1]
    ah_scr[rim:2 * rim, :] = embed(halo_ref[halo_right:halo_right + rim, :])[1]

    copies[1].wait()
    unit = 1.0 / (math.sqrt(head) * math.log(2.0))

    @pl.loop(0, width // tile)
    def _(j):
        at = pl.ds(pl.multiple_of(j * tile, tile), tile)
        at_k = pl.ds(pl.multiple_of(width + j * tile, tile), tile)
        at_v = pl.ds(pl.multiple_of(2 * width + j * tile, tile), tile)
        a = a_scr[...]
        ah = ah_scr[...]
        q_scr[:, at] = (dot(a, w_qkv[:, at]) * unit).astype(BF16)
        k_scr[rim:rim + rows, at] = dot(a, w_qkv[:, at_k]).astype(BF16)
        v_scr[rim:rim + rows, at] = dot(a, w_qkv[:, at_v]).astype(BF16)
        kh = dot(ah, w_qkv[:, at_k]).astype(BF16)
        k_scr[0:rim, at] = kh[:rim]
        k_scr[rim + rows:, at] = kh[rim:]
        vh = dot(ah, w_qkv[:, at_v]).astype(BF16)
        v_scr[0:rim, at] = vh[:rim]
        v_scr[rim + rows:, at] = vh[rim:]

    lane = lax.broadcasted_iota(jnp.int32, (LANES, LANES), 1)
    first = lane < head

    @pl.loop(0, rows // LANES)
    def _(i):
        at = pl.ds(pl.multiple_of(i * LANES, LANES), LANES)
        window = pl.ds(pl.multiple_of(i * LANES, LANES), keys)
        qm = qmask[...]
        km = kmask[...]
        ones = jnp.ones((keys, LANES), BF16)
        zero = jnp.zeros((LANES, LANES), BF16)
        for p in range(width // LANES):
            cols = slice(p * LANES, (p + 1) * LANES)
            q = q_scr[at, cols]
            qx = jnp.concatenate(
                [
                    jnp.concatenate([jnp.where(first, q, zero), qm], axis=1),
                    jnp.concatenate([jnp.where(first, zero, q), qm], axis=1),
                ],
                axis=0,
            )
            kx = jnp.concatenate([k_scr[window, cols], km], axis=1)
            s = dot_t(qx, kx)
            e = jnp.exp2(s - jnp.max(s, axis=-1, keepdims=True)).astype(BF16)
            vx = jnp.concatenate([v_scr[window, cols], ones], axis=1)
            o = dot(e, vx)
            num = jnp.where(first, o[:LANES, :LANES], o[LANES:, :LANES])
            den = jnp.where(first, o[:LANES, LANES:], o[LANES:, LANES:])
            o_scr[at, cols] = (num / den).astype(BF16)

    copies[2].wait()

    @pl.loop(0, width // tile)
    def _(j):
        at = pl.ds(pl.multiple_of(j * tile, tile), tile)
        h_scr[:, at] += mods_ref[2:3, at] * dot(o_scr[...], w_proj[:, at])

    @pl.loop(0, rows // part)
    def _(i):
        at = pl.ds(pl.multiple_of(i * part, part), part)
        a_scr[at, :] = (layer_norm(h_scr[at, :]) * scale2 + shift2).astype(BF16)

    copies[3].wait()

    @pl.loop(0, w_up.shape[1] // tile)
    def _(j):
        at = pl.ds(pl.multiple_of(j * tile, tile), tile)
        g_scr[:, at] = gelu(dot(a_scr[...], w_up[:, at])).astype(BF16)

    copies[4].wait()

    @pl.loop(0, width // tile)
    def _(j):
        at = pl.ds(pl.multiple_of(j * tile, tile), tile)
        h_scr[:, at] += mods_ref[5:6, at] * dot(g_scr[...], w_down[:, at])

    copies[5].wait()
    step = step_ref[0]

    @pl.loop(0, rows // part)
    def _(i):
        at = pl.ds(pl.multiple_of(i * part, part), part)
        inc_ref[at, :] = step * dot(layer_norm(h_scr[at, :]).astype(BF16), w_out[...])


def sweep(own, halo, halo_right, halo_left, mods, step, weights):
    w_in, w_qkv, w_proj, w_up, w_down, w_out = weights
    rows, channels = own.shape
    width, wide = w_up.shape
    rim = REACH * GY * GZ
    full = rows + 2 * rim
    vmem = pl.BlockSpec(memory_space=pltpu.VMEM)
    hbm = pl.BlockSpec(memory_space=pl.ANY)
    scratch = [pltpu.VMEM(w.shape, w.dtype) for w in weights]
    scratch += [
        pltpu.VMEM((rows, width), F32),
        pltpu.VMEM((rows, width), BF16),
        pltpu.VMEM((2 * rim, width), BF16),
        pltpu.VMEM((rows, width), BF16),
        pltpu.VMEM((full, width), BF16),
        pltpu.VMEM((full, width), BF16),
        pltpu.VMEM((rows, width), BF16),
        pltpu.VMEM((rows, wide), BF16),
        pltpu.VMEM((LANES, LANES), BF16),
        pltpu.VMEM(((2 * REACH + 2) * GY * GZ, LANES), BF16),
        pltpu.SemaphoreType.DMA((len(weights),)),
    ]
    flops = 2 * rows * width * (4 * width + 2 * wide)
    return pl.pallas_call(
        functools.partial(sweep_kernel, halo_right, halo_left),
        in_specs=[vmem, vmem, vmem, pl.BlockSpec(memory_space=pltpu.SMEM)] + [hbm] * 6,
        out_specs=vmem,
        out_shape=jax.ShapeDtypeStruct((rows, channels), F32),
        scratch_shapes=scratch,
        compiler_params=pltpu.CompilerParams(vmem_limit_bytes=48 << 20),
        cost_estimate=pl.CostEstimate(
            flops=flops, bytes_accessed=sum(w.size * 2 for w in weights), transcendentals=0
        ),
        name="sweep",
    )(own, halo, mods, step, *weights)


def rim_of_neighbours(field):
    count = lax.axis_size("gx")
    rows = field.shape[0]
    rim = REACH * GY * GZ
    if count == 2:
        other = lax.ppermute(field, "gx", [(0, 1), (1, 0)])
        return other, 0, rows - rim
    right = lax.ppermute(field[:rim], "gx", [((i + 1) % count, i) for i in range(count)])
    left = lax.ppermute(field[-rim:], "gx", [(i, (i + 1) % count) for i in range(count)])
    return jnp.concatenate([right, left]), 0, rim


def ahead(x, distance):
    count = lax.axis_size("win")
    return lax.ppermute(x, "win", [(i + distance, i) for i in range(count - distance)])


def behind(x, distance):
    count = lax.axis_size("win")
    return lax.ppermute(x, "win", [(i, i + distance) for i in range(count - distance)])


def slid(state, offset):
    count = lax.axis_size("win")
    place = lax.axis_index("win")
    final = state
    distance = 1
    while distance < count:
        moved = ahead(state, distance)
        if 2 * distance < count:
            span = [(count - 1 - i, count - 1 - i - distance) for i in range(distance)]
            spread = lax.ppermute(final, "win", span)
        taken = jnp.where(place + distance < count, moved, final)
        state = jnp.where((offset & distance) != 0, taken, state)
        if 2 * distance < count:
            newly = (place >= count - 2 * distance) & (place < count - distance)
            final = jnp.where(newly, spread, final)
        distance *= 2
    return state


def local(
    prev_states, timesteps, step_sizes, slide,
    w_time, w_ada, w_in, w_qkv, w_proj, w_up, w_down, w_out,
):
    count = lax.axis_size("win")
    place = lax.axis_index("win")
    offset = slide[0] - 1
    mods = modulation(timesteps[0], w_time, w_ada)
    weights = (w_in, w_qkv[0], w_proj[0], w_up[0], w_down[0], w_out)
    state = slid(prev_states[0], offset)
    opening = jnp.where(place == 0, state, 0.0)
    field = state.astype(BF16)
    for sweep_index in range(SWEEPS):
        halo, right, left = rim_of_neighbours(field)
        inc = sweep(field, halo, right, left, mods, step_sizes, weights)
        total = inc + opening
        distance = 1
        while distance < count:
            total = total + behind(total, distance)
            distance *= 2
        field = jnp.where(place == 0, state, total - inc).astype(BF16)
    return total[None]


def solution(mesh):
    in_specs = (
        P(("groups", "win"), "gx", None), P(("groups", "win")), P(("groups", "win")),
        P(), P(), P(), P(), P(), P(), P(), P(), P(),
    )
    out_specs = P(("groups", "win"), "gx", None)
    return jax.shard_map(local, mesh=mesh, in_specs=in_specs, out_specs=out_specs, check_vma=False)
```

```python
import functools
import math

import jax
import jax.numpy as jnp
from jax import lax
from jax.experimental import pallas as pl
from jax.experimental.pallas import tpu as pltpu
from jax.sharding import PartitionSpec as P

HEADS = 12
SWEEPS = 2
GY = 8
GZ = 8
REACH = 3
EPSILON = 1e-06
FAR = -(2.0**100)
LANES = 128
F32 = jnp.float32
BF16 = jnp.bfloat16


def dot(a, b):
    return lax.dot_general(a, b, (((1,), (0,)), ((), ())), preferred_element_type=F32)


def dot_t(a, b):
    return lax.dot_general(a, b, (((1,), (1,)), ((), ())), preferred_element_type=F32)


def layer_norm(values):
    centred = values - jnp.mean(values, axis=-1, keepdims=True)
    spread = jnp.mean(centred * centred, axis=-1, keepdims=True)
    return centred * lax.rsqrt(spread + EPSILON)


def silu(x):
    return x / (1.0 + jnp.exp(-x))


def gelu(x):
    inner = x * (math.sqrt(2.0 / math.pi) + (math.sqrt(2.0 / math.pi) * 0.044715) * (x * x))
    half = 0.5 * x
    return half + half * jnp.tanh(inner)


def mods_kernel(emb_ref, w_time_ref, w_ada_ref, out_ref):
    condition = silu(dot(emb_ref[...], w_time_ref[...]))
    active = silu(condition).astype(BF16)
    out_ref[...] = dot(active, w_ada_ref[...])


def modulation(moment, w_time, w_ada):
    half = w_time.shape[0] // 2
    freqs = jnp.exp(-math.log(10000.0) * jnp.arange(half, dtype=F32) / half)
    angles = moment.astype(F32) * freqs
    embedded = jnp.concatenate([jnp.cos(angles), jnp.sin(angles)]).astype(BF16)
    embedded = jnp.broadcast_to(embedded[None], (8, embedded.shape[0]))
    depth, wide = w_ada.shape[1:]
    steps = 6
    out = pl.pallas_call(
        mods_kernel,
        grid=(steps,),
        in_specs=[
            pl.BlockSpec(embedded.shape, lambda i: (0, 0)),
            pl.BlockSpec(w_time.shape, lambda i: (0, 0)),
            pl.BlockSpec((depth, wide // steps), lambda i: (0, i)),
        ],
        out_specs=pl.BlockSpec((8, wide // steps), lambda i: (0, i)),
        out_shape=jax.ShapeDtypeStruct((8, wide), F32),
        compiler_params=pltpu.CompilerParams(vmem_limit_bytes=16 << 20),
        name="mods",
    )(embedded, w_time, w_ada[0])
    return out[0].reshape(6, -1)


def sweep_kernel(
    halo_right, halo_left,
    own_ref, halo_ref, mods_ref, step_ref,
    w_in_hbm, w_qkv_hbm, w_proj_hbm, w_up_hbm, w_down_hbm, w_out_hbm,
    inc_ref,
    w_in, w_qkv, w_proj, w_up, w_down, w_out,
    h_scr, a_scr, ah_scr, q_scr, k_scr, v_scr, o_scr, g_scr, qmask, kmask, sems,
):
    pairs = (
        (w_in_hbm, w_in), (w_qkv_hbm, w_qkv), (w_proj_hbm, w_proj),
        (w_up_hbm, w_up), (w_down_hbm, w_down), (w_out_hbm, w_out),
    )
    copies = [pltpu.make_async_copy(s, d, sems.at[i]) for i, (s, d) in enumerate(pairs)]
    for c in copies:
        c.start()
    rows, width = h_scr.shape
    rim = REACH * GY * GZ
    head = width // HEADS
    tile = 256
    shift1, scale1, gate1 = mods_ref[0:1, :], 1.0 + mods_ref[1:2, :], mods_ref[2:3, :]
    shift2, scale2, gate2 = mods_ref[3:4, :], 1.0 + mods_ref[4:5, :], mods_ref[5:6, :]

    r = lax.broadcasted_iota(jnp.int32, (LANES, LANES), 0)
    f = lax.broadcasted_iota(jnp.int32, (LANES, LANES), 1)
    cell = r % (GY * GZ)
    hit = (
        (f == cell // GZ) | (f == GY + cell % GZ) | (f == GY + GZ + r // (GY * GZ))
    )
    qmask[...] = jnp.where(hit, FAR, 0.0).astype(BF16)
    keys = kmask.shape[0]
    r = lax.broadcasted_iota(jnp.int32, (keys, LANES), 0)
    f = lax.broadcasted_iota(jnp.int32, (keys, LANES), 1)
    cell = r % (GY * GZ)
    plane = r // (GY * GZ)
    hit = (
        (f == (cell // GZ + GY // 2) % GY)
        | (f == GY + (cell % GZ + GZ // 2) % GZ)
        | ((f == GY + GZ) & (plane == 2 * REACH + 1))
        | ((f == GY + GZ + 1) & (plane == 0))
    )
    kmask[...] = jnp.where(hit, 1.0, 0.0).astype(BF16)

    copies[0].wait()

    def embed(x):
        h = dot(x, w_in[...])
        return h, (layer_norm(h) * scale1 + shift1).astype(BF16)

    part = 128

    @pl.loop(0, rows // part)
    def _(i):
        at = pl.ds(pl.multiple_of(i * part, part), part)
        h, a = embed(own_ref[at, :])
        h_scr[at, :] = h
        a_scr[at, :] = a

    ah_scr[0:rim, :] = embed(halo_ref[halo_left:halo_left + rim, :])[1]
    ah_scr[rim:2 * rim, :] = embed(halo_ref[halo_right:halo_right + rim, :])[1]

    copies[1].wait()
    unit = 1.0 / (math.sqrt(head) * math.log(2.0))

    @pl.loop(0, width // tile)
    def _(j):
        at = pl.ds(pl.multiple_of(j * tile, tile), tile)
        at_k = pl.ds(pl.multiple_of(width + j * tile, tile), tile)
        at_v = pl.ds(pl.multiple_of(2 * width + j * tile, tile), tile)
        a = a_scr[...]
        ah = ah_scr[...]
        q_scr[:, at] = (dot(a, w_qkv[:, at]) * unit).astype(BF16)
        k_scr[rim:rim + rows, at] = dot(a, w_qkv[:, at_k]).astype(BF16)
        v_scr[rim:rim + rows, at] = dot(a, w_qkv[:, at_v]).astype(BF16)
        kh = dot(ah, w_qkv[:, at_k]).astype(BF16)
        k_scr[0:rim, at] = kh[:rim]
        k_scr[rim + rows:, at] = kh[rim:]
        vh = dot(ah, w_qkv[:, at_v]).astype(BF16)
        v_scr[0:rim, at] = vh[:rim]
        v_scr[rim + rows:, at] = vh[rim:]

    lane = lax.broadcasted_iota(jnp.int32, (LANES, LANES), 1)
    first = lane < head

    @pl.loop(0, rows // LANES)
    def _(i):
        at = pl.ds(pl.multiple_of(i * LANES, LANES), LANES)
        window = pl.ds(pl.multiple_of(i * LANES, LANES), keys)
        qm = qmask[...]
        km = kmask[...]
        ones = jnp.ones((keys, LANES), BF16)
        zero = jnp.zeros((LANES, LANES), BF16)
        for p in range(width // LANES):
            cols = slice(p * LANES, (p + 1) * LANES)
            q = q_scr[at, cols]
            qx = jnp.concatenate(
                [
                    jnp.concatenate([jnp.where(first, q, zero), qm], axis=1),
                    jnp.concatenate([jnp.where(first, zero, q), qm], axis=1),
                ],
                axis=0,
            )
            kx = jnp.concatenate([k_scr[window, cols], km], axis=1)
            s = dot_t(qx, kx)
            e = jnp.exp2(s - jnp.max(s, axis=-1, keepdims=True)).astype(BF16)
            vx = jnp.concatenate([v_scr[window, cols], ones], axis=1)
            o = dot(e, vx)
            num = jnp.where(first, o[:LANES, :LANES], o[LANES:, :LANES])
            den = jnp.where(first, o[:LANES, LANES:], o[LANES:, LANES:])
            o_scr[at, cols] = (num / den).astype(BF16)

    copies[2].wait()

    @pl.loop(0, width // tile)
    def _(j):
        at = pl.ds(pl.multiple_of(j * tile, tile), tile)
        h_scr[:, at] += mods_ref[2:3, at] * dot(o_scr[...], w_proj[:, at])

    @pl.loop(0, rows // part)
    def _(i):
        at = pl.ds(pl.multiple_of(i * part, part), part)
        a_scr[at, :] = (layer_norm(h_scr[at, :]) * scale2 + shift2).astype(BF16)

    copies[3].wait()

    @pl.loop(0, w_up.shape[1] // tile)
    def _(j):
        at = pl.ds(pl.multiple_of(j * tile, tile), tile)
        g_scr[:, at] = gelu(dot(a_scr[...], w_up[:, at])).astype(BF16)

    copies[4].wait()

    @pl.loop(0, width // tile)
    def _(j):
        at = pl.ds(pl.multiple_of(j * tile, tile), tile)
        h_scr[:, at] += mods_ref[5:6, at] * dot(g_scr[...], w_down[:, at])

    copies[5].wait()
    step = step_ref[0]

    @pl.loop(0, rows // part)
    def _(i):
        at = pl.ds(pl.multiple_of(i * part, part), part)
        out = step * dot(layer_norm(h_scr[at, :]).astype(BF16), w_out[...])
        inc_ref[at, :] = out.astype(BF16)


def sweep(own, halo, halo_right, halo_left, mods, step, weights):
    w_in, w_qkv, w_proj, w_up, w_down, w_out = weights
    rows, channels = own.shape
    width, wide = w_up.shape
    rim = REACH * GY * GZ
    full = rows + 2 * rim
    vmem = pl.BlockSpec(memory_space=pltpu.VMEM)
    hbm = pl.BlockSpec(memory_space=pl.ANY)
    scratch = [pltpu.VMEM(w.shape, w.dtype) for w in weights]
    scratch += [
        pltpu.VMEM((rows, width), F32),
        pltpu.VMEM((rows, width), BF16),
        pltpu.VMEM((2 * rim, width), BF16),
        pltpu.VMEM((rows, width), BF16),
        pltpu.VMEM((full, width), BF16),
        pltpu.VMEM((full, width), BF16),
        pltpu.VMEM((rows, width), BF16),
        pltpu.VMEM((rows, wide), BF16),
        pltpu.VMEM((LANES, LANES), BF16),
        pltpu.VMEM(((2 * REACH + 2) * GY * GZ, LANES), BF16),
        pltpu.SemaphoreType.DMA((len(weights),)),
    ]
    flops = 2 * rows * width * (4 * width + 2 * wide)
    return pl.pallas_call(
        functools.partial(sweep_kernel, halo_right, halo_left),
        in_specs=[vmem, vmem, vmem, pl.BlockSpec(memory_space=pltpu.SMEM)] + [hbm] * 6,
        out_specs=vmem,
        out_shape=jax.ShapeDtypeStruct((rows, channels), BF16),
        scratch_shapes=scratch,
        compiler_params=pltpu.CompilerParams(vmem_limit_bytes=48 << 20),
        cost_estimate=pl.CostEstimate(
            flops=flops, bytes_accessed=sum(w.size * 2 for w in weights), transcendentals=0
        ),
        name="sweep",
    )(own, halo, mods, step, *weights)


def rim_of_neighbours(field):
    count = lax.axis_size("gx")
    rows = field.shape[0]
    rim = REACH * GY * GZ
    if count == 2:
        other = lax.ppermute(field, "gx", [(0, 1), (1, 0)])
        return other, 0, rows - rim
    right = lax.ppermute(field[:rim], "gx", [((i + 1) % count, i) for i in range(count)])
    left = lax.ppermute(field[-rim:], "gx", [(i, (i + 1) % count) for i in range(count)])
    return jnp.concatenate([right, left]), 0, rim


def exchange(pieces):
    return lax.all_to_all(pieces, "win", 0, 0)


def choose_kernel(offset_ref, states_ref, fields_ref, start_ref):
    count = states_ref.shape[0]
    offset = offset_ref[0]
    start_ref[...] = states_ref[offset]
    for k in range(count):
        fields_ref[k] = states_ref[jnp.minimum(k + offset, count - 1)].astype(BF16)


def advance_kernel(inc_ref, start_ref, fields_ref):
    total = start_ref[...]
    for k in range(inc_ref.shape[0]):
        fields_ref[k] = total.astype(BF16)
        total = total + inc_ref[k].astype(F32)


def close_kernel(inc_ref, start_ref, fields_ref, gap_ref):
    total = start_ref[...]
    for k in range(inc_ref.shape[0]):
        total = total + inc_ref[k].astype(F32)
        gap_ref[k] = (total - fields_ref[k].astype(F32)).astype(BF16)


def small_call(kernel, name, args, out_shape):
    vmem = pl.BlockSpec(memory_space=pltpu.VMEM)
    smem = pl.BlockSpec(memory_space=pltpu.SMEM)
    return pl.pallas_call(
        kernel,
        in_specs=[smem if x.dtype == jnp.int32 else vmem for x in args],
        out_specs=jax.tree.map(lambda _: vmem, out_shape),
        out_shape=out_shape,
        compiler_params=pltpu.CompilerParams(vmem_limit_bytes=8 << 20),
        name=name,
    )(*args)


def local(
    prev_states, timesteps, step_sizes, slide,
    w_time, w_ada, w_in, w_qkv, w_proj, w_up, w_down, w_out,
):
    count = lax.axis_size("win")
    rows, channels = prev_states.shape[1:]
    cut = (count, rows // count, channels)
    mods = modulation(timesteps[0], w_time, w_ada)
    weights = (w_in, w_qkv[0], w_proj[0], w_up[0], w_down[0], w_out)
    states = exchange(prev_states.reshape(cut))
    of_fields = jax.ShapeDtypeStruct(cut, BF16)
    fields, start = small_call(
        choose_kernel, "choose", (slide - 1, states),
        (of_fields, jax.ShapeDtypeStruct(cut[1:], F32)),
    )
    for sweep_index in range(SWEEPS):
        field = exchange(fields).reshape(rows, channels)
        halo, right, left = rim_of_neighbours(field)
        inc = sweep(field, halo, right, left, mods, step_sizes, weights)
        incs = exchange(inc.reshape(cut))
        if sweep_index + 1 < SWEEPS:
            fields = small_call(advance_kernel, "advance", (incs, start), of_fields)
    gap = exchange(small_call(close_kernel, "close", (incs, start, fields), of_fields))
    return (field.astype(F32) + gap.reshape(rows, channels).astype(F32))[None]


def solution(mesh):
    in_specs = (
        P(("groups", "win"), "gx", None), P(("groups", "win")), P(("groups", "win")),
        P(), P(), P(), P(), P(), P(), P(), P(), P(),
    )
    out_specs = P(("groups", "win"), "gx", None)
    return jax.shard_map(local, mesh=mesh, in_specs=in_specs, out_specs=out_specs, check_vma=False)
```

```python
import functools
import math

import jax
import jax.numpy as jnp
from jax import lax
from jax.experimental import pallas as pl
from jax.experimental.pallas import tpu as pltpu
from jax.sharding import PartitionSpec as P

HEADS = 12
SWEEPS = 2
GY = 8
GZ = 8
REACH = 3
EPSILON = 1e-06
FAR = -(2.0**100)
LANES = 128
VMEM_LIMIT = 28 << 20
F32 = jnp.float32
BF16 = jnp.bfloat16


def dot(a, b):
    return lax.dot_general(a, b, (((1,), (0,)), ((), ())), preferred_element_type=F32)


def dot_t(a, b):
    return lax.dot_general(a, b, (((1,), (1,)), ((), ())), preferred_element_type=F32)


def layer_norm(values):
    centred = values - jnp.mean(values, axis=-1, keepdims=True)
    spread = jnp.mean(centred * centred, axis=-1, keepdims=True)
    return centred * lax.rsqrt(spread + EPSILON)


def silu(x):
    return x / (1.0 + jnp.exp(-x))


def gelu(x):
    inner = x * (math.sqrt(2.0 / math.pi) + (math.sqrt(2.0 / math.pi) * 0.044715) * (x * x))
    half = 0.5 * x
    return half + half * jnp.tanh(inner)


def modulation_kernel(emb_ref, w_time_hbm, w_ada_hbm, mods_ref, w_time, w_ada, sems):
    parts, _, wide = w_ada.shape
    first = pltpu.make_async_copy(w_time_hbm, w_time, sems.at[0])
    first.start()
    blocks = []
    for i in range(parts):
        block = w_ada_hbm.at[:, pl.ds(i * wide, wide)]
        blocks.append(pltpu.make_async_copy(block, w_ada.at[i], sems.at[1 + i]))
        blocks[-1].start()
    first.wait()
    condition = silu(dot(emb_ref[...], w_time[...]))
    active = silu(condition).astype(BF16)
    for i in range(parts):
        blocks[i].wait()
        mods_ref[i] = dot(active, w_ada[i])


def in_hbm(x):
    return pltpu.with_memory_space_constraint(x, pltpu.HBM)


def modulation(moment, w_time, w_ada):
    half = w_time.shape[0] // 2
    freqs = jnp.exp(-math.log(10000.0) * jnp.arange(half, dtype=F32) / half)
    angles = moment.astype(F32) * freqs
    embedded = jnp.concatenate([jnp.cos(angles), jnp.sin(angles)]).astype(BF16)
    embedded = jnp.broadcast_to(embedded[None], (8, embedded.shape[0]))
    parts = 6
    depth, wide = w_ada.shape
    vmem = pl.BlockSpec(memory_space=pltpu.VMEM)
    hbm = pl.BlockSpec(memory_space=pltpu.HBM)
    return pl.pallas_call(
        modulation_kernel,
        in_specs=[vmem, hbm, hbm],
        out_specs=vmem,
        out_shape=jax.ShapeDtypeStruct((parts, 8, wide // parts), F32),
        scratch_shapes=[
            pltpu.VMEM(w_time.shape, w_time.dtype),
            pltpu.VMEM((parts, depth, wide // parts), w_ada.dtype),
            pltpu.SemaphoreType.DMA((1 + parts,)),
        ],
        compiler_params=pltpu.CompilerParams(vmem_limit_bytes=16 << 20),
        cost_estimate=pl.CostEstimate(
            flops=16 * w_ada.size, bytes_accessed=2 * w_ada.size, transcendentals=0
        ),
        name="modulation",
    )(embedded, in_hbm(w_time), in_hbm(w_ada))


def first_sweep_kernel(halo_right, halo_left, *refs):
    fields, sources, incs, kept, rest = refs[:4], refs[4:10], refs[10:12], refs[12:18], refs[18:]
    scratch, sems = rest[:-1], rest[-1]
    copies = []
    for i, (source, target) in enumerate(zip(sources, kept)):
        copies.append(pltpu.make_async_copy(source, target, sems.at[i]))
        copies[-1].start()
    sweep_kernel(halo_right, halo_left, *fields, *kept, *incs, *scratch, arrived=copies)


def sweep_kernel(
    halo_right, halo_left,
    own_ref, halo_ref, mods_ref, step_ref,
    w_in, w_qkv, w_proj, w_up, w_down, w_out,
    inc_ref, own_inc_ref,
    h_scr, a_scr, ah_scr, q_scr, k_scr, v_scr, o_scr, g_scr, qmask, kmask,
    arrived=None,
):
    def need(i):
        if arrived is not None:
            arrived[i].wait()

    rows, width = h_scr.shape
    rim = REACH * GY * GZ
    head = width // HEADS
    tile = 256
    shift1, scale1 = mods_ref[0, 0:1, :], 1.0 + mods_ref[1, 0:1, :]
    shift2, scale2 = mods_ref[3, 0:1, :], 1.0 + mods_ref[4, 0:1, :]

    def place_of(shape):
        r = lax.broadcasted_iota(jnp.int32, shape, 0)
        f = lax.broadcasted_iota(jnp.int32, shape, 1)
        return f, r // (GY * GZ), (r // GZ) % GY, r % GZ

    f, plane, y, z = place_of(qmask.shape)
    hit = (f == y) | (f == GY + z) | (f == GY + GZ + plane)
    qmask[...] = jnp.where(hit, FAR, 0.0).astype(BF16)
    keys = kmask.shape[0]
    f, plane, y, z = place_of((GY * GZ, LANES))
    hit = (f == (y + GY // 2) % GY) | (f == GY + (z + GZ // 2) % GZ)
    near = jnp.where(hit, 1.0, 0.0).astype(BF16)
    end = jnp.where(f == GY + GZ, 1.0, 0.0).astype(BF16)
    start = jnp.where(f == GY + GZ + 1, 1.0, 0.0).astype(BF16)
    for p in range(2 * REACH + 2):
        more = {0: start, 2 * REACH + 1: end}.get(p)
        kmask[p * GY * GZ:(p + 1) * GY * GZ, :] = near if more is None else near + more

    need(0)
    def embed(x):
        h = dot(x, w_in[...])
        return h, (layer_norm(h) * scale1 + shift1).astype(BF16)

    part = 128

    @pl.loop(0, rows // part)
    def _(i):
        at = pl.ds(pl.multiple_of(i * part, part), part)
        h, a = embed(own_ref[at, :])
        h_scr[at, :] = h
        a_scr[at, :] = a

    ah_scr[0:rim, :] = embed(halo_ref[halo_left:halo_left + rim, :])[1]
    ah_scr[rim:2 * rim, :] = embed(halo_ref[halo_right:halo_right + rim, :])[1]

    need(1)
    unit = 1.0 / (math.sqrt(head) * math.log(2.0))

    @pl.loop(0, width // tile)
    def _(j):
        at = pl.ds(pl.multiple_of(j * tile, tile), tile)
        at_k = pl.ds(pl.multiple_of(width + j * tile, tile), tile)
        at_v = pl.ds(pl.multiple_of(2 * width + j * tile, tile), tile)
        a = a_scr[...]
        ah = ah_scr[...]
        q_scr[:, at] = (dot(a, w_qkv[:, at]) * unit).astype(BF16)
        k_scr[rim:rim + rows, at] = dot(a, w_qkv[:, at_k]).astype(BF16)
        v_scr[rim:rim + rows, at] = dot(a, w_qkv[:, at_v]).astype(BF16)
        kh = dot(ah, w_qkv[:, at_k]).astype(BF16)
        k_scr[0:rim, at] = kh[:rim]
        k_scr[rim + rows:, at] = kh[rim:]
        vh = dot(ah, w_qkv[:, at_v]).astype(BF16)
        v_scr[0:rim, at] = vh[:rim]
        v_scr[rim + rows:, at] = vh[rim:]

    lane = lax.broadcasted_iota(jnp.int32, (LANES, LANES), 1)
    first = lane < head

    @pl.loop(0, rows // LANES)
    def _(i):
        at = pl.ds(pl.multiple_of(i * LANES, LANES), LANES)
        window = pl.ds(pl.multiple_of(i * LANES, LANES), keys)
        qm = qmask[...]
        km = kmask[...]
        ones = jnp.ones((keys, LANES), BF16)
        zero = jnp.zeros((LANES, LANES), BF16)
        for p in range(width // LANES):
            cols = slice(p * LANES, (p + 1) * LANES)
            q = q_scr[at, cols]
            qx = jnp.concatenate(
                [
                    jnp.concatenate([jnp.where(first, q, zero), qm], axis=1),
                    jnp.concatenate([jnp.where(first, zero, q), qm], axis=1),
                ],
                axis=0,
            )
            kx = jnp.concatenate([k_scr[window, cols], km], axis=1)
            s = dot_t(qx, kx)
            e = jnp.exp2(s - jnp.max(s, axis=-1, keepdims=True)).astype(BF16)
            vx = jnp.concatenate([v_scr[window, cols], ones], axis=1)
            o = dot(e, vx)
            num = jnp.where(first, o[:LANES, :LANES], o[LANES:, :LANES])
            den = jnp.where(first, o[:LANES, LANES:], o[LANES:, LANES:])
            o_scr[at, cols] = (num / den).astype(BF16)

    need(2)
    @pl.loop(0, width // tile)
    def _(j):
        at = pl.ds(pl.multiple_of(j * tile, tile), tile)
        h_scr[:, at] += mods_ref[2, 0:1, at] * dot(o_scr[...], w_proj[:, at])

    @pl.loop(0, rows // part)
    def _(i):
        at = pl.ds(pl.multiple_of(i * part, part), part)
        a_scr[at, :] = (layer_norm(h_scr[at, :]) * scale2 + shift2).astype(BF16)

    need(3)
    @pl.loop(0, w_up.shape[1] // tile)
    def _(j):
        at = pl.ds(pl.multiple_of(j * tile, tile), tile)
        g_scr[:, at] = gelu(dot(a_scr[...], w_up[:, at])).astype(BF16)

    need(4)
    @pl.loop(0, width // tile)
    def _(j):
        at = pl.ds(pl.multiple_of(j * tile, tile), tile)
        h_scr[:, at] += mods_ref[5, 0:1, at] * dot(g_scr[...], w_down[:, at])

    need(5)
    step = step_ref[0]

    @pl.loop(0, rows // part)
    def _(i):
        at = pl.ds(pl.multiple_of(i * part, part), part)
        out = step * dot(layer_norm(h_scr[at, :]).astype(BF16), w_out[...])
        inc_ref[at, :] = out.astype(BF16)
        own_inc_ref[at, :] = out


def sweep(own, halo, halo_right, halo_left, mods, step, weights, first):
    rows, channels = own.shape
    width, wide = weights[3].shape
    rim = REACH * GY * GZ
    full = rows + 2 * rim
    vmem = pl.BlockSpec(memory_space=pltpu.VMEM)
    hbm = pl.BlockSpec(memory_space=pltpu.HBM)
    scratch = [
        pltpu.VMEM((rows, width), F32),
        pltpu.VMEM((rows, width), BF16),
        pltpu.VMEM((2 * rim, width), BF16),
        pltpu.VMEM((rows, width), BF16),
        pltpu.VMEM((full, width), BF16),
        pltpu.VMEM((full, width), BF16),
        pltpu.VMEM((rows, width), BF16),
        pltpu.VMEM((rows, wide), BF16),
        pltpu.VMEM((LANES, LANES), BF16),
        pltpu.VMEM(((2 * REACH + 2) * GY * GZ, LANES), BF16),
    ]
    out_shape = [
        jax.ShapeDtypeStruct((rows, channels), BF16),
        jax.ShapeDtypeStruct((rows, channels), F32),
    ]
    kernel = sweep_kernel
    if first:
        kernel = first_sweep_kernel
        scratch.append(pltpu.SemaphoreType.DMA((len(weights),)))
        out_shape += [pltpu.VMEM(w.shape, w.dtype) for w in weights]
        weights = tuple(in_hbm(w) for w in weights)
    inc, own_inc, *kept = pl.pallas_call(
        functools.partial(kernel, halo_right, halo_left),
        in_specs=[vmem, vmem, vmem, pl.BlockSpec(memory_space=pltpu.SMEM)]
        + [hbm if first else vmem] * len(weights),
        out_specs=[vmem] * len(out_shape),
        out_shape=out_shape,
        scratch_shapes=scratch,
        compiler_params=pltpu.CompilerParams(vmem_limit_bytes=VMEM_LIMIT),
        cost_estimate=pl.CostEstimate(
            flops=2 * rows * width * (4 * width + 2 * wide),
            bytes_accessed=sum(w.size * 2 for w in weights),
            transcendentals=0,
        ),
        name="first_sweep" if first else "sweep",
    )(own, halo, mods, step, *weights)
    return inc, own_inc, tuple(kept) if first else weights


def rim_of_neighbours(field):
    count = lax.axis_size("gx")
    rows = field.shape[0]
    rim = REACH * GY * GZ
    if count == 2:
        other = lax.ppermute(field, "gx", [(0, 1), (1, 0)])
        return other, 0, rows - rim
    right = lax.ppermute(field[:rim], "gx", [((i + 1) % count, i) for i in range(count)])
    left = lax.ppermute(field[-rim:], "gx", [(i, (i + 1) % count) for i in range(count)])
    return jnp.concatenate([right, left]), 0, rim


def exchange(pieces):
    return lax.all_to_all(pieces, "win", 0, 0)


def choose_kernel(offset_ref, states_ref, fields_ref, start_ref):
    count = states_ref.shape[0]
    offset = offset_ref[0]
    start_ref[...] = states_ref[offset]
    for k in range(count):
        fields_ref[k] = states_ref[jnp.minimum(k + offset, count - 1)].astype(BF16)


def advance_kernel(inc_ref, start_ref, fields_ref):
    total = start_ref[...]
    for k in range(inc_ref.shape[0]):
        fields_ref[k] = total.astype(BF16)
        total = total + inc_ref[k].astype(F32)


def close_kernel(inc_ref, start_ref, fields_ref, gap_ref):
    total = start_ref[...]
    for k in range(inc_ref.shape[0]):
        gap_ref[k] = (total - fields_ref[k].astype(F32)).astype(BF16)
        total = total + inc_ref[k].astype(F32)


def small_call(kernel, name, args, out_shape):
    vmem = pl.BlockSpec(memory_space=pltpu.VMEM)
    smem = pl.BlockSpec(memory_space=pltpu.SMEM)
    return pl.pallas_call(
        kernel,
        in_specs=[smem if x.dtype == jnp.int32 else vmem for x in args],
        out_specs=jax.tree.map(lambda _: vmem, out_shape),
        out_shape=out_shape,
        compiler_params=pltpu.CompilerParams(vmem_limit_bytes=8 << 20),
        name=name,
    )(*args)


def local(
    prev_states, timesteps, step_sizes, slide,
    w_time, w_ada, w_in, w_qkv, w_proj, w_up, w_down, w_out,
):
    count = lax.axis_size("win")
    rows, channels = prev_states.shape[1:]
    cut = (count, rows // count, channels)
    weights = (w_in, w_qkv[0], w_proj[0], w_up[0], w_down[0], w_out)
    mods = modulation(timesteps[0], w_time, w_ada[0])
    states = exchange(prev_states.reshape(cut))
    states, mods = lax.optimization_barrier((states, mods))
    of_fields = jax.ShapeDtypeStruct(cut, BF16)
    fields, start = small_call(
        choose_kernel, "choose", (slide - 1, states),
        (of_fields, jax.ShapeDtypeStruct(cut[1:], F32)),
    )
    for sweep_index in range(SWEEPS):
        field = exchange(fields).reshape(rows, channels)
        halo, right, left = rim_of_neighbours(field)
        inc, own_inc, weights = sweep(
            field, halo, right, left, mods, step_sizes, weights, sweep_index == 0
        )
        incs = exchange(inc.reshape(cut))
        if sweep_index + 1 < SWEEPS:
            fields = small_call(advance_kernel, "advance", (incs, start), of_fields)
    gap = exchange(small_call(close_kernel, "close", (incs, start, fields), of_fields))
    gap = gap.reshape(rows, channels).astype(F32)
    return (field.astype(F32) + gap + own_inc)[None]


def solution(mesh):
    in_specs = (
        P(("groups", "win"), "gx", None), P(("groups", "win")), P(("groups", "win")),
        P(), P(), P(), P(), P(), P(), P(), P(), P(),
    )
    out_specs = P(("groups", "win"), "gx", None)
    return jax.shard_map(local, mesh=mesh, in_specs=in_specs, out_specs=out_specs, check_vma=False)
```

```python
import functools
import math

import jax
import jax.numpy as jnp
from jax import lax
from jax.experimental import pallas as pl
from jax.experimental.pallas import tpu as pltpu
from jax.sharding import PartitionSpec as P

HEADS = 12
SWEEPS = 2
GY = 8
GZ = 8
REACH = 3
EPSILON = 1e-06
FAR = -(2.0**100)
LANES = 128
VMEM_LIMIT = 28 << 20
EMBED_PART = 128
QKV_TILE = 768
LEAD = 1
ATT_UNROLL = 4
PROJ_PART = 512
UP_TILE = 1536
DOWN_PART = 512
F32 = jnp.float32
BF16 = jnp.bfloat16


def dot(a, b):
    return lax.dot_general(a, b, (((1,), (0,)), ((), ())), preferred_element_type=F32)


def dot_t(a, b):
    return lax.dot_general(a, b, (((1,), (1,)), ((), ())), preferred_element_type=F32)


def layer_norm(values):
    centred = values - jnp.mean(values, axis=-1, keepdims=True)
    spread = jnp.mean(centred * centred, axis=-1, keepdims=True)
    return centred * lax.rsqrt(spread + EPSILON)


def silu(x):
    return x / (1.0 + jnp.exp(-x))


def gelu(x):
    inner = x * (math.sqrt(2.0 / math.pi) + (math.sqrt(2.0 / math.pi) * 0.044715) * (x * x))
    half = 0.5 * x
    return half + half * jnp.tanh(inner)


def modulation_kernel(emb_ref, w_time_hbm, w_ada_hbm, mods_ref, w_time, w_ada, sems):
    parts, _, wide = w_ada.shape
    first = pltpu.make_async_copy(w_time_hbm, w_time, sems.at[0])
    first.start()
    blocks = []
    for i in range(parts):
        block = w_ada_hbm.at[:, pl.ds(i * wide, wide)]
        blocks.append(pltpu.make_async_copy(block, w_ada.at[i], sems.at[1 + i]))
        blocks[-1].start()
    first.wait()
    condition = silu(dot(emb_ref[...], w_time[...]))
    active = silu(condition).astype(BF16)
    for i in range(parts):
        blocks[i].wait()
        mods_ref[i] = dot(active, w_ada[i])


def in_hbm(x):
    return pltpu.with_memory_space_constraint(x, pltpu.HBM)


def modulation(moment, w_time, w_ada):
    half = w_time.shape[0] // 2
    freqs = jnp.exp(-math.log(10000.0) * jnp.arange(half, dtype=F32) / half)
    angles = moment.astype(F32) * freqs
    embedded = jnp.concatenate([jnp.cos(angles), jnp.sin(angles)]).astype(BF16)
    embedded = jnp.broadcast_to(embedded[None], (8, embedded.shape[0]))
    parts = 6
    depth, wide = w_ada.shape
    vmem = pl.BlockSpec(memory_space=pltpu.VMEM)
    hbm = pl.BlockSpec(memory_space=pltpu.HBM)
    return pl.pallas_call(
        modulation_kernel,
        in_specs=[vmem, hbm, hbm],
        out_specs=vmem,
        out_shape=jax.ShapeDtypeStruct((parts, 8, wide // parts), F32),
        scratch_shapes=[
            pltpu.VMEM(w_time.shape, w_time.dtype),
            pltpu.VMEM((parts, depth, wide // parts), w_ada.dtype),
            pltpu.SemaphoreType.DMA((1 + parts,)),
        ],
        compiler_params=pltpu.CompilerParams(vmem_limit_bytes=16 << 20),
        cost_estimate=pl.CostEstimate(
            flops=16 * w_ada.size, bytes_accessed=2 * w_ada.size, transcendentals=0
        ),
        name="modulation",
    )(embedded, in_hbm(w_time), in_hbm(w_ada))


def first_sweep_kernel(halo_right, halo_left, *refs):
    fields, sources, incs, kept, rest = refs[:4], refs[4:10], refs[10:12], refs[12:18], refs[18:]
    scratch, sems = rest[:-1], rest[-1]
    copies = []
    for i, (source, target) in enumerate(zip(sources, kept)):
        copies.append(pltpu.make_async_copy(source, target, sems.at[i]))
        copies[-1].start()
    sweep_kernel(halo_right, halo_left, *fields, *kept, *incs, *scratch, arrived=copies)


def sweep_kernel(
    halo_right, halo_left,
    own_ref, halo_ref, mods_ref, step_ref,
    w_in, w_qkv, w_proj, w_up, w_down, w_out,
    inc_ref, own_inc_ref,
    h_scr, a_scr, b_scr, q_scr, k_scr, v_scr, o_scr, g_scr, qmask, kmask,
    arrived=None,
):
    def need(i):
        if arrived is not None:
            arrived[i].wait()

    rows, width = h_scr.shape
    rim = REACH * GY * GZ
    head = width // HEADS
    shift1, scale1 = mods_ref[0, 0:1, :], 1.0 + mods_ref[1, 0:1, :]
    shift2, scale2 = mods_ref[3, 0:1, :], 1.0 + mods_ref[4, 0:1, :]

    def place_of(shape):
        r = lax.broadcasted_iota(jnp.int32, shape, 0)
        f = lax.broadcasted_iota(jnp.int32, shape, 1)
        return f, r // (GY * GZ), (r // GZ) % GY, r % GZ

    f, plane, y, z = place_of(qmask.shape)
    hit = (f == y) | (f == GY + z) | (f == GY + GZ + plane)
    qmask[...] = jnp.where(hit, FAR, 0.0).astype(BF16)
    keys = kmask.shape[0]
    f, plane, y, z = place_of((GY * GZ, LANES))
    hit = (f == (y + GY // 2) % GY) | (f == GY + (z + GZ // 2) % GZ)
    near = jnp.where(hit, 1.0, 0.0).astype(BF16)
    end = jnp.where(f == GY + GZ, 1.0, 0.0).astype(BF16)
    start = jnp.where(f == GY + GZ + 1, 1.0, 0.0).astype(BF16)
    for p in range(2 * REACH + 2):
        more = {0: start, 2 * REACH + 1: end}.get(p)
        kmask[p * GY * GZ:(p + 1) * GY * GZ, :] = near if more is None else near + more

    need(0)
    def embed(x):
        h = dot(x, w_in[...])
        return h, (layer_norm(h) * scale1 + shift1).astype(BF16)

    a_scr[0:rim, :] = embed(halo_ref[halo_left:halo_left + rim, :])[1]
    a_scr[rim + rows:, :] = embed(halo_ref[halo_right:halo_right + rim, :])[1]
    for i in range(0, rows, EMBED_PART):
        h_scr[i:i + EMBED_PART, :], a_scr[rim + i:rim + i + EMBED_PART, :] = embed(
            own_ref[i:i + EMBED_PART, :]
        )

    need(1)
    unit = 1.0 / (math.sqrt(head) * math.log(2.0))

    @pl.loop(0, width // QKV_TILE)
    def _(j):
        at = pl.ds(pl.multiple_of(j * QKV_TILE, QKV_TILE), QKV_TILE)
        at_k = pl.ds(pl.multiple_of(width + j * QKV_TILE, QKV_TILE), QKV_TILE)
        at_v = pl.ds(pl.multiple_of(2 * width + j * QKV_TILE, QKV_TILE), QKV_TILE)
        q_scr[:, at] = (dot(a_scr[rim:rim + rows, :], w_qkv[:, at]) * unit).astype(BF16)
        k_scr[:, at] = dot(a_scr[...], w_qkv[:, at_k]).astype(BF16)
        v_scr[:, at] = dot(a_scr[...], w_qkv[:, at_v]).astype(BF16)

    lane = lax.broadcasted_iota(jnp.int32, (LANES, LANES), 1)
    first = lane < head

    @pl.loop(0, rows // LANES, unroll=ATT_UNROLL)
    def _(i):
        at = pl.ds(pl.multiple_of(i * LANES, LANES), LANES)
        window = pl.ds(pl.multiple_of(i * LANES, LANES), keys)
        qm = qmask[...]
        km = kmask[...]
        ones = jnp.ones((keys, LANES), BF16)
        zero = jnp.zeros((LANES, LANES), BF16)

        def scores(p):
            cols = slice(p * LANES, (p + 1) * LANES)
            q = q_scr[at, cols]
            qx = jnp.concatenate(
                [
                    jnp.concatenate([jnp.where(first, q, zero), qm], axis=1),
                    jnp.concatenate([jnp.where(first, zero, q), qm], axis=1),
                ],
                axis=0,
            )
            return dot_t(qx, jnp.concatenate([k_scr[window, cols], km], axis=1))

        def mix(p, s):
            cols = slice(p * LANES, (p + 1) * LANES)
            e = jnp.exp2(s - jnp.max(s, axis=-1, keepdims=True)).astype(BF16)
            o = dot(e, jnp.concatenate([v_scr[window, cols], ones], axis=1))
            num = jnp.where(first, o[:LANES, :LANES], o[LANES:, :LANES])
            den = jnp.where(first, o[:LANES, LANES:], o[LANES:, LANES:])
            o_scr[at, cols] = (num / den).astype(BF16)

        units = width // LANES
        waiting = [scores(p) for p in range(LEAD)]
        for p in range(units):
            if p + LEAD < units:
                waiting.append(scores(p + LEAD))
            mix(p, waiting.pop(0))

    need(2)
    for i in range(0, rows, PROJ_PART):
        at = slice(i, i + PROJ_PART)
        h = h_scr[at, :] + mods_ref[2, 0:1, :] * dot(o_scr[at, :], w_proj[...])
        h_scr[at, :] = h
        b_scr[at, :] = (layer_norm(h) * scale2 + shift2).astype(BF16)

    need(3)

    @pl.loop(0, w_up.shape[1] // UP_TILE)
    def _(j):
        at = pl.ds(pl.multiple_of(j * UP_TILE, UP_TILE), UP_TILE)
        g_scr[:, at] = gelu(dot(b_scr[...], w_up[:, at])).astype(BF16)

    need(4)
    need(5)
    step = step_ref[0]
    for i in range(0, rows, DOWN_PART):
        at = slice(i, i + DOWN_PART)
        h = h_scr[at, :] + mods_ref[5, 0:1, :] * dot(g_scr[at, :], w_down[...])
        out = step * dot(layer_norm(h).astype(BF16), w_out[...])
        inc_ref[at, :] = out.astype(BF16)
        own_inc_ref[at, :] = out


def sweep(own, halo, halo_right, halo_left, mods, step, weights, first):
    rows, channels = own.shape
    width, wide = weights[3].shape
    rim = REACH * GY * GZ
    full = rows + 2 * rim
    vmem = pl.BlockSpec(memory_space=pltpu.VMEM)
    hbm = pl.BlockSpec(memory_space=pltpu.HBM)
    scratch = [
        pltpu.VMEM((rows, width), F32),
        pltpu.VMEM((full, width), BF16),
        pltpu.VMEM((rows, width), BF16),
        pltpu.VMEM((rows, width), BF16),
        pltpu.VMEM((full, width), BF16),
        pltpu.VMEM((full, width), BF16),
        pltpu.VMEM((rows, width), BF16),
        pltpu.VMEM((rows, wide), BF16),
        pltpu.VMEM((LANES, LANES), BF16),
        pltpu.VMEM(((2 * REACH + 2) * GY * GZ, LANES), BF16),
    ]
    out_shape = [
        jax.ShapeDtypeStruct((rows, channels), BF16),
        jax.ShapeDtypeStruct((rows, channels), F32),
    ]
    kernel = sweep_kernel
    if first:
        kernel = first_sweep_kernel
        scratch.append(pltpu.SemaphoreType.DMA((len(weights),)))
        out_shape += [pltpu.VMEM(w.shape, w.dtype) for w in weights]
        weights = tuple(in_hbm(w) for w in weights)
    inc, own_inc, *kept = pl.pallas_call(
        functools.partial(kernel, halo_right, halo_left),
        in_specs=[vmem, vmem, vmem, pl.BlockSpec(memory_space=pltpu.SMEM)]
        + [hbm if first else vmem] * len(weights),
        out_specs=[vmem] * len(out_shape),
        out_shape=out_shape,
        scratch_shapes=scratch,
        compiler_params=pltpu.CompilerParams(vmem_limit_bytes=VMEM_LIMIT),
        cost_estimate=pl.CostEstimate(
            flops=2 * rows * width * (4 * width + 2 * wide),
            bytes_accessed=sum(w.size * 2 for w in weights),
            transcendentals=0,
        ),
        name="first_sweep" if first else "sweep",
    )(own, halo, mods, step, *weights)
    return inc, own_inc, tuple(kept) if first else weights


def rim_of_neighbours(field):
    count = lax.axis_size("gx")
    rows = field.shape[0]
    rim = REACH * GY * GZ
    if count == 2:
        other = lax.ppermute(field, "gx", [(0, 1), (1, 0)])
        return other, 0, rows - rim
    right = lax.ppermute(field[:rim], "gx", [((i + 1) % count, i) for i in range(count)])
    left = lax.ppermute(field[-rim:], "gx", [(i, (i + 1) % count) for i in range(count)])
    return jnp.concatenate([right, left]), 0, rim


def exchange(pieces):
    return lax.all_to_all(pieces, "win", 0, 0)


def choose_kernel(offset_ref, states_ref, fields_ref, start_ref):
    count = states_ref.shape[0]
    offset = offset_ref[0]
    start_ref[...] = states_ref[offset]
    for k in range(count):
        fields_ref[k] = states_ref[jnp.minimum(k + offset, count - 1)].astype(BF16)


def advance_kernel(inc_ref, start_ref, fields_ref):
    total = start_ref[...]
    for k in range(inc_ref.shape[0]):
        fields_ref[k] = total.astype(BF16)
        total = total + inc_ref[k].astype(F32)


def close_kernel(inc_ref, start_ref, fields_ref, gap_ref):
    total = start_ref[...]
    for k in range(inc_ref.shape[0]):
        gap_ref[k] = (total - fields_ref[k].astype(F32)).astype(BF16)
        total = total + inc_ref[k].astype(F32)


def small_call(kernel, name, args, out_shape):
    vmem = pl.BlockSpec(memory_space=pltpu.VMEM)
    smem = pl.BlockSpec(memory_space=pltpu.SMEM)
    return pl.pallas_call(
        kernel,
        in_specs=[smem if x.dtype == jnp.int32 else vmem for x in args],
        out_specs=jax.tree.map(lambda _: vmem, out_shape),
        out_shape=out_shape,
        compiler_params=pltpu.CompilerParams(vmem_limit_bytes=8 << 20),
        name=name,
    )(*args)


def local(
    prev_states, timesteps, step_sizes, slide,
    w_time, w_ada, w_in, w_qkv, w_proj, w_up, w_down, w_out,
):
    count = lax.axis_size("win")
    rows, channels = prev_states.shape[1:]
    cut = (count, rows // count, channels)
    weights = (w_in, w_qkv[0], w_proj[0], w_up[0], w_down[0], w_out)
    mods = modulation(timesteps[0], w_time, w_ada[0])
    states = exchange(prev_states.reshape(cut))
    states, mods = lax.optimization_barrier((states, mods))
    of_fields = jax.ShapeDtypeStruct(cut, BF16)
    fields, start = small_call(
        choose_kernel, "choose", (slide - 1, states),
        (of_fields, jax.ShapeDtypeStruct(cut[1:], F32)),
    )
    for sweep_index in range(SWEEPS):
        field = exchange(fields).reshape(rows, channels)
        halo, right, left = rim_of_neighbours(field)
        inc, own_inc, weights = sweep(
            field, halo, right, left, mods, step_sizes, weights, sweep_index == 0
        )
        incs = exchange(inc.reshape(cut))
        if sweep_index + 1 < SWEEPS:
            fields = small_call(advance_kernel, "advance", (incs, start), of_fields)
    gap = exchange(small_call(close_kernel, "close", (incs, start, fields), of_fields))
    gap = gap.reshape(rows, channels).astype(F32)
    return (field.astype(F32) + gap + own_inc)[None]


def solution(mesh):
    in_specs = (
        P(("groups", "win"), "gx", None), P(("groups", "win")), P(("groups", "win")),
        P(), P(), P(), P(), P(), P(), P(), P(), P(),
    )
    out_specs = P(("groups", "win"), "gx", None)
    return jax.shard_map(local, mesh=mesh, in_specs=in_specs, out_specs=out_specs, check_vma=False)
```

```python
import functools
import math

import jax
import jax.numpy as jnp
from jax import lax
from jax.experimental import pallas as pl
from jax.experimental.pallas import tpu as pltpu
from jax.sharding import PartitionSpec as P

HEADS = 12
SWEEPS = 2
GY = 8
GZ = 8
REACH = 3
EPSILON = 1e-06
FAR = -(2.0**100)
LANES = 128
VMEM_LIMIT = 28 << 20
EMBED_PART = 128
QKV_TILE = 768
LEAD = 1
ATT_UNROLL = 4
PROJ_PART = 512
UP_TILE = 1536
DOWN_PART = 512
EARLY = 2
F32 = jnp.float32
BF16 = jnp.bfloat16


def dot(a, b):
    return lax.dot_general(a, b, (((1,), (0,)), ((), ())), preferred_element_type=F32)


def dot_t(a, b):
    return lax.dot_general(a, b, (((1,), (1,)), ((), ())), preferred_element_type=F32)


def layer_norm(values):
    centred = values - jnp.mean(values, axis=-1, keepdims=True)
    spread = jnp.mean(centred * centred, axis=-1, keepdims=True)
    return centred * lax.rsqrt(spread + EPSILON)


def silu(x):
    return x / (1.0 + jnp.exp(-x))


def gelu_of_half(half):
    rate = math.sqrt(2.0 / math.pi)
    inner = half * (2.0 * rate + (8.0 * rate * 0.044715) * (half * half))
    return half + half * jnp.tanh(inner)


def modulation_kernel(emb_ref, w_time_hbm, w_ada_hbm, mods_ref, w_time, w_ada, sems):
    parts, _, wide = w_ada.shape
    first = pltpu.make_async_copy(w_time_hbm, w_time, sems.at[0])
    first.start()
    blocks = []
    for i in range(parts):
        block = w_ada_hbm.at[:, pl.ds(i * wide, wide)]
        blocks.append(pltpu.make_async_copy(block, w_ada.at[i], sems.at[1 + i]))
        blocks[-1].start()
    first.wait()
    condition = silu(dot(emb_ref[...], w_time[...]))
    active = silu(condition).astype(BF16)
    for i in range(parts):
        blocks[i].wait()
        mods_ref[i] = dot(active, w_ada[i])


def in_hbm(x):
    return pltpu.with_memory_space_constraint(x, pltpu.HBM)


def modulation(moment, w_time, w_ada):
    half = w_time.shape[0] // 2
    freqs = jnp.exp(-math.log(10000.0) * jnp.arange(half, dtype=F32) / half)
    angles = moment.astype(F32) * freqs
    embedded = jnp.concatenate([jnp.cos(angles), jnp.sin(angles)]).astype(BF16)
    embedded = jnp.broadcast_to(embedded[None], (8, embedded.shape[0]))
    parts = 6
    depth, wide = w_ada.shape
    vmem = pl.BlockSpec(memory_space=pltpu.VMEM)
    hbm = pl.BlockSpec(memory_space=pltpu.HBM)
    return pl.pallas_call(
        modulation_kernel,
        in_specs=[vmem, hbm, hbm],
        out_specs=vmem,
        out_shape=jax.ShapeDtypeStruct((parts, 8, wide // parts), F32),
        scratch_shapes=[
            pltpu.VMEM(w_time.shape, w_time.dtype),
            pltpu.VMEM((parts, depth, wide // parts), w_ada.dtype),
            pltpu.SemaphoreType.DMA((1 + parts,)),
        ],
        compiler_params=pltpu.CompilerParams(vmem_limit_bytes=16 << 20),
        cost_estimate=pl.CostEstimate(
            flops=16 * w_ada.size, bytes_accessed=2 * w_ada.size, transcendentals=0
        ),
        name="modulation",
    )(embedded, in_hbm(w_time), in_hbm(w_ada))


def first_sweep_kernel(halo_right, halo_left, *refs):
    fields, sources, incs, kept, rest = refs[:4], refs[4:10], refs[10:11], refs[11:17], refs[17:]
    scratch, sems = rest[:-1], rest[-1]
    copies = [
        pltpu.make_async_copy(source, target, sems.at[i])
        for i, (source, target) in enumerate(zip(sources, kept))
    ]
    for i in range(EARLY):
        copies[i].start()
    sweep_kernel(halo_right, halo_left, *fields, *kept, *incs, *scratch, arrived=copies)


def sweep_kernel(
    halo_right, halo_left,
    own_ref, halo_ref, mods_ref, step_ref,
    w_in, w_qkv, w_proj, w_up, w_down, w_out,
    inc_ref,
    h_scr, a_scr, b_scr, q_scr, k_scr, v_scr, o_scr, g_scr, qmask, kmask,
    arrived=None,
):
    def need(i):
        if arrived is not None:
            arrived[i].wait()
            if i == EARLY - 1:
                for copy in arrived[EARLY:]:
                    copy.start()

    rows, width = h_scr.shape
    rim = REACH * GY * GZ
    head = width // HEADS
    shift1, scale1 = mods_ref[0, 0:1, :], 1.0 + mods_ref[1, 0:1, :]
    shift2, scale2 = 0.5 * mods_ref[3, 0:1, :], 0.5 + 0.5 * mods_ref[4, 0:1, :]

    def place_of(shape):
        r = lax.broadcasted_iota(jnp.int32, shape, 0)
        f = lax.broadcasted_iota(jnp.int32, shape, 1)
        return f, r // (GY * GZ), (r // GZ) % GY, r % GZ

    f, plane, y, z = place_of(qmask.shape)
    hit = (f == y) | (f == GY + z) | (f == GY + GZ + plane)
    qmask[...] = jnp.where(hit, FAR, 0.0).astype(BF16)
    keys = kmask.shape[0]
    f, plane, y, z = place_of((GY * GZ, LANES))
    hit = (f == (y + GY // 2) % GY) | (f == GY + (z + GZ // 2) % GZ)
    near = jnp.where(hit, 1.0, 0.0).astype(BF16)
    end = jnp.where(f == GY + GZ, 1.0, 0.0).astype(BF16)
    start = jnp.where(f == GY + GZ + 1, 1.0, 0.0).astype(BF16)
    for p in range(2 * REACH + 2):
        more = {0: start, 2 * REACH + 1: end}.get(p)
        kmask[p * GY * GZ:(p + 1) * GY * GZ, :] = near if more is None else near + more

    need(0)

    def embed(x):
        h = dot(x, w_in[...])
        return h, (layer_norm(h) * scale1 + shift1).astype(BF16)

    a_scr[0:rim, :] = embed(halo_ref[halo_left:halo_left + rim, :])[1]
    a_scr[rim + rows:, :] = embed(halo_ref[halo_right:halo_right + rim, :])[1]
    for i in range(0, rows, EMBED_PART):
        h_scr[i:i + EMBED_PART, :], a_scr[rim + i:rim + i + EMBED_PART, :] = embed(
            own_ref[i:i + EMBED_PART, :]
        )

    need(1)
    unit = 1.0 / (math.sqrt(head) * math.log(2.0))

    @pl.loop(0, width // QKV_TILE)
    def _(j):
        at = pl.ds(pl.multiple_of(j * QKV_TILE, QKV_TILE), QKV_TILE)
        at_k = pl.ds(pl.multiple_of(width + j * QKV_TILE, QKV_TILE), QKV_TILE)
        at_v = pl.ds(pl.multiple_of(2 * width + j * QKV_TILE, QKV_TILE), QKV_TILE)
        q_scr[:, at] = (dot(a_scr[rim:rim + rows, :], w_qkv[:, at]) * unit).astype(BF16)
        k_scr[:, at] = dot(a_scr[...], w_qkv[:, at_k]).astype(BF16)
        v_scr[:, at] = dot(a_scr[...], w_qkv[:, at_v]).astype(BF16)

    lane = lax.broadcasted_iota(jnp.int32, (LANES, LANES), 1)
    first = lane < head

    @pl.loop(0, rows // LANES, unroll=ATT_UNROLL)
    def _(i):
        at = pl.ds(pl.multiple_of(i * LANES, LANES), LANES)
        window = pl.ds(pl.multiple_of(i * LANES, LANES), keys)
        qm = qmask[...]
        km = kmask[...]
        ones = jnp.ones((keys, LANES), BF16)
        zero = jnp.zeros((LANES, LANES), BF16)

        def scores(p):
            cols = slice(p * LANES, (p + 1) * LANES)
            q = q_scr[at, cols]
            qx = jnp.concatenate(
                [
                    jnp.concatenate([jnp.where(first, q, zero), qm], axis=1),
                    jnp.concatenate([jnp.where(first, zero, q), qm], axis=1),
                ],
                axis=0,
            )
            return dot_t(qx, jnp.concatenate([k_scr[window, cols], km], axis=1))

        def mix(p, s):
            cols = slice(p * LANES, (p + 1) * LANES)
            e = jnp.exp2(s - jnp.max(s, axis=-1, keepdims=True)).astype(BF16)
            o = dot(e, jnp.concatenate([v_scr[window, cols], ones], axis=1))
            num = jnp.where(first, o[:LANES, :LANES], o[LANES:, :LANES])
            den = jnp.where(first, o[:LANES, LANES:], o[LANES:, LANES:])
            o_scr[at, cols] = (num / den).astype(BF16)

        units = width // LANES
        waiting = [scores(p) for p in range(LEAD)]
        for p in range(units):
            if p + LEAD < units:
                waiting.append(scores(p + LEAD))
            mix(p, waiting.pop(0))

    need(2)
    for i in range(0, rows, PROJ_PART):
        at = slice(i, i + PROJ_PART)
        h = h_scr[at, :] + mods_ref[2, 0:1, :] * dot(o_scr[at, :], w_proj[...])
        h_scr[at, :] = h
        b_scr[at, :] = (layer_norm(h) * scale2 + shift2).astype(BF16)

    need(3)

    @pl.loop(0, w_up.shape[1] // UP_TILE)
    def _(j):
        at = pl.ds(pl.multiple_of(j * UP_TILE, UP_TILE), UP_TILE)
        g_scr[:, at] = gelu_of_half(dot(b_scr[...], w_up[:, at])).astype(BF16)

    need(4)
    need(5)
    step = step_ref[0]
    for i in range(0, rows, DOWN_PART):
        at = slice(i, i + DOWN_PART)
        h = h_scr[at, :] + mods_ref[5, 0:1, :] * dot(g_scr[at, :], w_down[...])
        out = step * dot(layer_norm(h).astype(BF16), w_out[...])
        inc_ref[at, :] = out


def sweep(own, halo, halo_right, halo_left, mods, step, weights, first):
    rows, channels = own.shape
    width, wide = weights[3].shape
    rim = REACH * GY * GZ
    full = rows + 2 * rim
    vmem = pl.BlockSpec(memory_space=pltpu.VMEM)
    hbm = pl.BlockSpec(memory_space=pltpu.HBM)
    scratch = [
        pltpu.VMEM((rows, width), F32),
        pltpu.VMEM((full, width), BF16),
        pltpu.VMEM((rows, width), BF16),
        pltpu.VMEM((rows, width), BF16),
        pltpu.VMEM((full, width), BF16),
        pltpu.VMEM((full, width), BF16),
        pltpu.VMEM((rows, width), BF16),
        pltpu.VMEM((rows, wide), BF16),
        pltpu.VMEM((LANES, LANES), BF16),
        pltpu.VMEM(((2 * REACH + 2) * GY * GZ, LANES), BF16),
    ]
    out_shape = [jax.ShapeDtypeStruct((rows, channels), F32)]
    kernel = sweep_kernel
    if first:
        kernel = first_sweep_kernel
        scratch.append(pltpu.SemaphoreType.DMA((len(weights),)))
        out_shape += [pltpu.VMEM(w.shape, w.dtype) for w in weights]
        weights = tuple(in_hbm(w) for w in weights)
    inc, *kept = pl.pallas_call(
        functools.partial(kernel, halo_right, halo_left),
        in_specs=[vmem, vmem, vmem, pl.BlockSpec(memory_space=pltpu.SMEM)]
        + [hbm if first else vmem] * len(weights),
        out_specs=[vmem] * len(out_shape),
        out_shape=out_shape,
        scratch_shapes=scratch,
        compiler_params=pltpu.CompilerParams(vmem_limit_bytes=VMEM_LIMIT),
        cost_estimate=pl.CostEstimate(
            flops=2 * rows * width * (4 * width + 2 * wide),
            bytes_accessed=sum(w.size * 2 for w in weights),
            transcendentals=0,
        ),
        name="first_sweep" if first else "sweep",
    )(own, halo, mods, step, *weights)
    return inc, tuple(kept) if first else weights


def rim_of_neighbours(field):
    count = lax.axis_size("gx")
    rows = field.shape[0]
    rim = REACH * GY * GZ
    if count == 2:
        other = lax.ppermute(field, "gx", [(0, 1), (1, 0)])
        return other, 0, rows - rim
    right = lax.ppermute(field[:rim], "gx", [((i + 1) % count, i) for i in range(count)])
    left = lax.ppermute(field[-rim:], "gx", [(i, (i + 1) % count) for i in range(count)])
    return jnp.concatenate([right, left]), 0, rim


def swap(x, distance):
    count = lax.axis_size("win")
    return lax.ppermute(x, "win", [(i, i ^ distance) for i in range(count)])


def together(*values):
    return lax.optimization_barrier(values)


def small_call(kernel, args, out_shape):
    vmem = pl.BlockSpec(memory_space=pltpu.VMEM)
    smem = pl.BlockSpec(memory_space=pltpu.SMEM)
    return pl.pallas_call(
        kernel,
        in_specs=[smem if x.dtype == jnp.int32 else vmem for x in args],
        out_specs=jax.tree.map(lambda _: vmem, out_shape),
        out_shape=out_shape,
        compiler_params=pltpu.CompilerParams(vmem_limit_bytes=4 << 20),
    )(*args)


def decisions(offset):
    count = lax.axis_size("win")
    place = lax.axis_index("win")
    bit = jnp.arange(count.bit_length() - 1, dtype=jnp.int32)
    distance = jnp.left_shift(1, bit)
    low = place & (distance - 1)
    mine = jnp.right_shift(place, bit) & 1
    lands = jnp.right_shift(mine * distance + low - offset, bit) & 1
    last = count // distance - 1 - jnp.right_shift(offset, bit)
    clamped = (low == distance - 1) & (jnp.right_shift(place, bit) >= last)
    keep = jnp.where(clamped, mine == 1, lands == mine)
    near = (jnp.right_shift(place ^ offset, bit) & 1) == 0
    return jnp.concatenate([keep, near, mine == 1]).astype(jnp.int32)


def pick(flags, flag, own, other):
    def kernel(flags_ref, own_ref, other_ref, out_ref):
        out_ref[...] = jnp.where(flags_ref[flag] != 0, own_ref[...], other_ref[...])

    return small_call(kernel, (flags, own, other), jax.ShapeDtypeStruct(own.shape, own.dtype))


def add_block(flags, flag, before, total, other):
    def kernel(flags_ref, *refs):
        *before_refs, total_ref, other_ref, before_out, total_out, sent_out = refs
        arrived = other_ref[...].astype(F32)
        mine = jnp.where(flags_ref[flag] != 0, arrived, 0.0)
        before_out[...] = before_refs[0][...] + mine if before_refs else mine
        sums = total_ref[...] + arrived
        total_out[...] = sums
        sent_out[...] = sums.astype(BF16)

    wide = jax.ShapeDtypeStruct(total.shape, F32)
    narrow = jax.ShapeDtypeStruct(total.shape, BF16)
    args = (flags,) + (() if before is None else (before,)) + (total, other)
    return small_call(kernel, args, (wide, wide, narrow))


def add_last(flags, flag, before, other, extra, kind):
    def kernel(flags_ref, before_ref, other_ref, *refs):
        mine = jnp.where(flags_ref[flag] != 0, other_ref[...].astype(F32), 0.0)
        total = before_ref[...] + mine
        for ref in refs[:-1]:
            total = total + ref[...]
        refs[-1][...] = total.astype(kind)

    return small_call(
        kernel, (flags, before, other) + extra,
        jax.ShapeDtypeStruct(before.shape, kind),
    )


def window_steps(
    prev_states, timesteps, step_sizes, slide,
    w_time, w_ada, w_in, w_qkv, w_proj, w_up, w_down, w_out,
):
    count = lax.axis_size("win")
    bits = count.bit_length() - 1
    assert count == 1 << bits and bits > 1, "window size"
    weights = (w_in, w_qkv[0], w_proj[0], w_up[0], w_down[0], w_out)
    flags = decisions(slide[0] - 1)
    mods = modulation(timesteps[0], w_time, w_ada[0])
    opening = prev_states[0]
    field = opening.astype(BF16)

    for bit in reversed(range(bits)):
        other = swap(field, 1 << bit)
        if bit == bits - 1:
            moved = swap(opening, 1)
            other, mods = together(other, mods)
        if bit == 0:
            field, opening, moved = together(field, opening, moved)
            opening = pick(flags, bits, opening, moved)
            moved = swap(opening, count // 2)
        field = pick(flags, bit, field, other)
    for sweep_index in range(SWEEPS):
        first = sweep_index == 0
        final = sweep_index == SWEEPS - 1
        halo, right, left = rim_of_neighbours(field)
        inc, weights = sweep(field, halo, right, left, mods, step_sizes, weights, first)
        if first:
            inc, opening, moved = together(inc, opening, moved)
            opening = pick(flags, 2 * bits - 1, opening, moved)
        before, total, sent = None, inc, inc.astype(BF16)
        for bit in range(bits - 1):
            other = swap(sent, 1 << bit)
            if first and bit + 1 < bits - 1:
                moved = swap(opening, 2 << bit)
                opening = pick(flags, bits + bit + 1, opening, moved)
            before, total, sent = add_block(flags, 2 * bits + bit, before, total, other)
        other = swap(sent, count // 2)
        field = add_last(
            flags, 3 * bits - 1, before, other, (opening, inc) if final else (opening,),
            F32 if final else BF16,
        )
    return field[None]


def solution(mesh):
    in_specs = (
        P(("groups", "win"), "gx", None), P(("groups", "win")), P(("groups", "win")),
        P(), P(), P(), P(), P(), P(), P(), P(), P(),
    )
    out_specs = P(("groups", "win"), "gx", None)
    return jax.shard_map(
        window_steps, mesh=mesh, in_specs=in_specs, out_specs=out_specs, check_vma=False
    )
```

```python
import functools
import math

import jax
import jax.numpy as jnp
from jax import lax
from jax.experimental import pallas as pl
from jax.experimental.pallas import tpu as pltpu
from jax.sharding import PartitionSpec as P

HEADS = 12
SWEEPS = 2
GY = 8
GZ = 8
REACH = 3
EPSILON = 1e-06
FAR = -(2.0**100)
LANES = 128
VMEM_LIMIT = 28 << 20
EMBED_PART = 128
QKV_TILE = 768
LEAD = 1
ATT_UNROLL = 4
PROJ_PART = 512
UP_TILE = 1536
DOWN_PART = 512
F32 = jnp.float32
BF16 = jnp.bfloat16


def dot(a, b):
    return lax.dot_general(a, b, (((1,), (0,)), ((), ())), preferred_element_type=F32)


def dot_t(a, b):
    return lax.dot_general(a, b, (((1,), (1,)), ((), ())), preferred_element_type=F32)


def layer_norm(values):
    centred = values - jnp.mean(values, axis=-1, keepdims=True)
    spread = jnp.mean(centred * centred, axis=-1, keepdims=True)
    return centred * lax.rsqrt(spread + EPSILON)


def silu(x):
    return x / (1.0 + jnp.exp(-x))


def gelu_of_half(half):
    rate = math.sqrt(2.0 / math.pi)
    inner = half * (2.0 * rate + (8.0 * rate * 0.044715) * (half * half))
    return half + half * jnp.tanh(inner)


def modulation_kernel(emb_ref, w_time_hbm, w_ada_hbm, mods_ref, w_time, w_ada, sems):
    parts, _, wide = w_ada.shape
    first = pltpu.make_async_copy(w_time_hbm, w_time, sems.at[0])
    first.start()
    blocks = []
    for i in range(parts):
        block = w_ada_hbm.at[:, pl.ds(i * wide, wide)]
        blocks.append(pltpu.make_async_copy(block, w_ada.at[i], sems.at[1 + i]))
        blocks[-1].start()
    first.wait()
    condition = silu(dot(emb_ref[...], w_time[...]))
    active = silu(condition).astype(BF16)
    for i in range(parts):
        blocks[i].wait()
        mods_ref[i] = dot(active, w_ada[i])


def in_hbm(x):
    return pltpu.with_memory_space_constraint(x, pltpu.HBM)


def load_kernel(*refs):
    count = len(refs) // 2
    sems = refs[-1]
    copies = [
        pltpu.make_async_copy(refs[i], refs[count + i], sems.at[i]) for i in range(count)
    ]
    for copy in copies:
        copy.start()
    for copy in copies:
        copy.wait()


def load(arrays):
    return tuple(
        pl.pallas_call(
            load_kernel,
            in_specs=[pl.BlockSpec(memory_space=pltpu.HBM)] * len(arrays),
            out_specs=[pl.BlockSpec(memory_space=pltpu.VMEM)] * len(arrays),
            out_shape=[pltpu.VMEM(x.shape, x.dtype) for x in arrays],
            scratch_shapes=[pltpu.SemaphoreType.DMA((len(arrays),))],
            compiler_params=pltpu.CompilerParams(vmem_limit_bytes=4 << 20),
            cost_estimate=pl.CostEstimate(
                flops=0, bytes_accessed=sum(2 * x.size for x in arrays), transcendentals=0
            ),
            name="load",
        )(*[in_hbm(x) for x in arrays])
    )


def modulation(moment, w_time, w_ada):
    half = w_time.shape[0] // 2
    freqs = jnp.exp(-math.log(10000.0) * jnp.arange(half, dtype=F32) / half)
    angles = moment.astype(F32) * freqs
    embedded = jnp.concatenate([jnp.cos(angles), jnp.sin(angles)]).astype(BF16)
    embedded = jnp.broadcast_to(embedded[None], (8, embedded.shape[0]))
    parts = 6
    depth, wide = w_ada.shape
    vmem = pl.BlockSpec(memory_space=pltpu.VMEM)
    hbm = pl.BlockSpec(memory_space=pltpu.HBM)
    return pl.pallas_call(
        modulation_kernel,
        in_specs=[vmem, hbm, hbm],
        out_specs=vmem,
        out_shape=jax.ShapeDtypeStruct((parts, 8, wide // parts), F32),
        scratch_shapes=[
            pltpu.VMEM(w_time.shape, w_time.dtype),
            pltpu.VMEM((parts, depth, wide // parts), w_ada.dtype),
            pltpu.SemaphoreType.DMA((1 + parts,)),
        ],
        compiler_params=pltpu.CompilerParams(vmem_limit_bytes=16 << 20),
        cost_estimate=pl.CostEstimate(
            flops=16 * w_ada.size, bytes_accessed=2 * w_ada.size, transcendentals=0
        ),
        name="modulation",
    )(embedded, in_hbm(w_time), in_hbm(w_ada))


def first_sweep_kernel(halo_right, halo_left, *refs):
    fields, ready, sources, (inc,), kept = refs[:4], refs[4:6], refs[6:10], refs[10:11], refs[11:15]
    scratch, sems = refs[15:-1], refs[-1]
    copies = [None] * len(ready)
    for i, (source, target) in enumerate(zip(sources, kept)):
        copies.append(pltpu.make_async_copy(source, target, sems.at[i]))
        copies[-1].start()
    sweep_kernel(halo_right, halo_left, *fields, *ready, *kept, inc, *scratch, arrived=copies)


def sweep_kernel(
    halo_right, halo_left,
    own_ref, halo_ref, mods_ref, step_ref,
    w_in, w_qkv, w_proj, w_up, w_down, w_out,
    inc_ref,
    h_scr, a_scr, b_scr, q_scr, k_scr, v_scr, o_scr, g_scr, qmask, kmask,
    arrived=None,
):
    def need(i):
        if arrived is not None and arrived[i] is not None:
            arrived[i].wait()

    rows, width = h_scr.shape
    rim = REACH * GY * GZ
    head = width // HEADS
    shift1, scale1 = mods_ref[0, 0:1, :], 1.0 + mods_ref[1, 0:1, :]
    shift2, scale2 = 0.5 * mods_ref[3, 0:1, :], 0.5 + 0.5 * mods_ref[4, 0:1, :]

    def place_of(shape):
        r = lax.broadcasted_iota(jnp.int32, shape, 0)
        f = lax.broadcasted_iota(jnp.int32, shape, 1)
        return f, r // (GY * GZ), (r // GZ) % GY, r % GZ

    f, plane, y, z = place_of(qmask.shape)
    hit = (f == y) | (f == GY + z) | (f == GY + GZ + plane)
    qmask[...] = jnp.where(hit, FAR, 0.0).astype(BF16)
    keys = kmask.shape[0]
    f, plane, y, z = place_of((GY * GZ, LANES))
    hit = (f == (y + GY // 2) % GY) | (f == GY + (z + GZ // 2) % GZ)
    near = jnp.where(hit, 1.0, 0.0).astype(BF16)
    end = jnp.where(f == GY + GZ, 1.0, 0.0).astype(BF16)
    start = jnp.where(f == GY + GZ + 1, 1.0, 0.0).astype(BF16)
    for p in range(2 * REACH + 2):
        more = {0: start, 2 * REACH + 1: end}.get(p)
        kmask[p * GY * GZ:(p + 1) * GY * GZ, :] = near if more is None else near + more

    need(0)

    def embed(x):
        h = dot(x, w_in[...])
        return h, (layer_norm(h) * scale1 + shift1).astype(BF16)

    a_scr[0:rim, :] = embed(halo_ref[halo_left:halo_left + rim, :])[1]
    a_scr[rim + rows:, :] = embed(halo_ref[halo_right:halo_right + rim, :])[1]
    for i in range(0, rows, EMBED_PART):
        h_scr[i:i + EMBED_PART, :], a_scr[rim + i:rim + i + EMBED_PART, :] = embed(
            own_ref[i:i + EMBED_PART, :]
        )

    need(1)
    unit = 1.0 / (math.sqrt(head) * math.log(2.0))

    @pl.loop(0, width // QKV_TILE)
    def _(j):
        at = pl.ds(pl.multiple_of(j * QKV_TILE, QKV_TILE), QKV_TILE)
        at_k = pl.ds(pl.multiple_of(width + j * QKV_TILE, QKV_TILE), QKV_TILE)
        at_v = pl.ds(pl.multiple_of(2 * width + j * QKV_TILE, QKV_TILE), QKV_TILE)
        q_scr[:, at] = (dot(a_scr[rim:rim + rows, :], w_qkv[:, at]) * unit).astype(BF16)
        k_scr[:, at] = dot(a_scr[...], w_qkv[:, at_k]).astype(BF16)
        v_scr[:, at] = dot(a_scr[...], w_qkv[:, at_v]).astype(BF16)

    lane = lax.broadcasted_iota(jnp.int32, (LANES, LANES), 1)
    first = lane < head

    @pl.loop(0, rows // LANES, unroll=ATT_UNROLL)
    def _(i):
        at = pl.ds(pl.multiple_of(i * LANES, LANES), LANES)
        window = pl.ds(pl.multiple_of(i * LANES, LANES), keys)
        qm = qmask[...]
        km = kmask[...]
        ones = jnp.ones((keys, LANES), BF16)
        zero = jnp.zeros((LANES, LANES), BF16)

        def scores(p):
            cols = slice(p * LANES, (p + 1) * LANES)
            q = q_scr[at, cols]
            qx = jnp.concatenate(
                [
                    jnp.concatenate([jnp.where(first, q, zero), qm], axis=1),
                    jnp.concatenate([jnp.where(first, zero, q), qm], axis=1),
                ],
                axis=0,
            )
            return dot_t(qx, jnp.concatenate([k_scr[window, cols], km], axis=1))

        def mix(p, s):
            cols = slice(p * LANES, (p + 1) * LANES)
            e = jnp.exp2(s - jnp.max(s, axis=-1, keepdims=True)).astype(BF16)
            o = dot(e, jnp.concatenate([v_scr[window, cols], ones], axis=1))
            num = jnp.where(first, o[:LANES, :LANES], o[LANES:, :LANES])
            den = jnp.where(first, o[:LANES, LANES:], o[LANES:, LANES:])
            o_scr[at, cols] = (num / den).astype(BF16)

        units = width // LANES
        waiting = [scores(p) for p in range(LEAD)]
        for p in range(units):
            if p + LEAD < units:
                waiting.append(scores(p + LEAD))
            mix(p, waiting.pop(0))

    need(2)
    for i in range(0, rows, PROJ_PART):
        at = slice(i, i + PROJ_PART)
        h = h_scr[at, :] + mods_ref[2, 0:1, :] * dot(o_scr[at, :], w_proj[...])
        h_scr[at, :] = h
        b_scr[at, :] = (layer_norm(h) * scale2 + shift2).astype(BF16)

    need(3)

    @pl.loop(0, w_up.shape[1] // UP_TILE)
    def _(j):
        at = pl.ds(pl.multiple_of(j * UP_TILE, UP_TILE), UP_TILE)
        g_scr[:, at] = gelu_of_half(dot(b_scr[...], w_up[:, at])).astype(BF16)

    need(4)
    need(5)
    step = step_ref[0]
    for i in range(0, rows, DOWN_PART):
        at = slice(i, i + DOWN_PART)
        h = h_scr[at, :] + mods_ref[5, 0:1, :] * dot(g_scr[at, :], w_down[...])
        out = step * dot(layer_norm(h).astype(BF16), w_out[...])
        inc_ref[at, :] = out


def sweep(own, halo, halo_right, halo_left, mods, step, weights, first):
    rows, channels = own.shape
    width, wide = weights[3].shape
    rim = REACH * GY * GZ
    full = rows + 2 * rim
    vmem = pl.BlockSpec(memory_space=pltpu.VMEM)
    hbm = pl.BlockSpec(memory_space=pltpu.HBM)
    scratch = [
        pltpu.VMEM((rows, width), F32),
        pltpu.VMEM((full, width), BF16),
        pltpu.VMEM((rows, width), BF16),
        pltpu.VMEM((rows, width), BF16),
        pltpu.VMEM((full, width), BF16),
        pltpu.VMEM((full, width), BF16),
        pltpu.VMEM((rows, width), BF16),
        pltpu.VMEM((rows, wide), BF16),
        pltpu.VMEM((LANES, LANES), BF16),
        pltpu.VMEM(((2 * REACH + 2) * GY * GZ, LANES), BF16),
    ]
    out_shape = [jax.ShapeDtypeStruct((rows, channels), F32)]
    kernel = sweep_kernel
    if first:
        kernel = first_sweep_kernel
        late = weights[2:]
        scratch.append(pltpu.SemaphoreType.DMA((len(late),)))
        out_shape += [pltpu.VMEM(w.shape, w.dtype) for w in late]
        weights = weights[:2] + tuple(in_hbm(w) for w in late)
    inc, *kept = pl.pallas_call(
        functools.partial(kernel, halo_right, halo_left),
        in_specs=[vmem, vmem, vmem, pl.BlockSpec(memory_space=pltpu.SMEM)]
        + [vmem] * 2
        + [hbm if first else vmem] * (len(weights) - 2),
        out_specs=[vmem] * len(out_shape),
        out_shape=out_shape,
        scratch_shapes=scratch,
        compiler_params=pltpu.CompilerParams(vmem_limit_bytes=VMEM_LIMIT),
        cost_estimate=pl.CostEstimate(
            flops=2 * rows * width * (4 * width + 2 * wide),
            bytes_accessed=sum(w.size * 2 for w in weights),
            transcendentals=0,
        ),
        name="first_sweep" if first else "sweep",
    )(own, halo, mods, step, *weights)
    return inc, weights[:2] + tuple(kept) if first else weights


def rim_of_neighbours(field):
    count = lax.axis_size("gx")
    rows = field.shape[0]
    rim = REACH * GY * GZ
    if count == 2:
        other = lax.ppermute(field, "gx", [(0, 1), (1, 0)])
        return other, 0, rows - rim
    right = lax.ppermute(field[:rim], "gx", [((i + 1) % count, i) for i in range(count)])
    left = lax.ppermute(field[-rim:], "gx", [(i, (i + 1) % count) for i in range(count)])
    return jnp.concatenate([right, left]), 0, rim


def swap(x, distance):
    count = lax.axis_size("win")
    return lax.ppermute(x, "win", [(i, i ^ distance) for i in range(count)])


def together(*values):
    return lax.optimization_barrier(values)


def small_call(kernel, args, out_shape):
    vmem = pl.BlockSpec(memory_space=pltpu.VMEM)
    return pl.pallas_call(
        kernel,
        in_specs=[vmem] * len(args),
        out_specs=jax.tree.map(lambda _: vmem, out_shape),
        out_shape=out_shape,
        compiler_params=pltpu.CompilerParams(vmem_limit_bytes=4 << 20),
    )(*args)


def decisions(offset, lanes):
    count = lax.axis_size("win")
    place = lax.axis_index("win")
    bit = jnp.arange(count.bit_length() - 1, dtype=jnp.int32)
    distance = jnp.left_shift(1, bit)
    low = place & (distance - 1)
    mine = jnp.right_shift(place, bit) & 1
    lands = jnp.right_shift(mine * distance + low - offset, bit) & 1
    last = count // distance - 1 - jnp.right_shift(offset, bit)
    clamped = (low == distance - 1) & (jnp.right_shift(place, bit) >= last)
    keep = jnp.where(clamped, mine == 1, lands == mine)
    near = (jnp.right_shift(place ^ offset, bit) & 1) == 0
    flags = jnp.concatenate([keep, near, mine == 1]).astype(jnp.int32)
    return jnp.broadcast_to(flags[:, None], (flags.shape[0], lanes))


def pick(flags, flag, own, other):
    def kernel(flags_ref, own_ref, other_ref, out_ref):
        own = flags_ref[flag:flag + 1, :] != 0
        out_ref[...] = jnp.where(own, own_ref[...], other_ref[...])

    return small_call(kernel, (flags, own, other), jax.ShapeDtypeStruct(own.shape, own.dtype))


def add_block(flags, flag, before, total, other, more):
    def kernel(flags_ref, *refs):
        refs = list(refs)
        start = refs.pop(0)[...] if before is not None else 0.0
        sums = refs[0][...]
        arrived = refs[1][...].astype(F32)
        above = flags_ref[flag:flag + 1, :] != 0
        refs[2][...] = start + jnp.where(above, arrived, 0.0)
        sums = sums + arrived
        refs[3][...] = sums.astype(BF16)
        if more:
            refs[4][...] = sums

    wide = jax.ShapeDtypeStruct(total.shape, F32)
    narrow = jax.ShapeDtypeStruct(total.shape, BF16)
    args = (flags,) + (() if before is None else (before,)) + (total, other)
    out = small_call(kernel, args, (wide, narrow) + ((wide,) if more else ()))
    return out if more else (*out, None)


def add_last(flags, flag, before, other, extra, kind):
    def kernel(flags_ref, before_ref, other_ref, *refs):
        above = flags_ref[flag:flag + 1, :] != 0
        mine = jnp.where(above, other_ref[...].astype(F32), 0.0)
        total = before_ref[...] + mine
        for ref in refs[:-1]:
            total = total + ref[...]
        refs[-1][...] = total.astype(kind)

    return small_call(
        kernel, (flags, before, other) + extra,
        jax.ShapeDtypeStruct(before.shape, kind),
    )


def window_steps(
    prev_states, timesteps, step_sizes, slide,
    w_time, w_ada, w_in, w_qkv, w_proj, w_up, w_down, w_out,
):
    count = lax.axis_size("win")
    bits = count.bit_length() - 1
    assert count == 1 << bits and bits > 1, "window size"
    weights = (w_in, w_qkv[0], w_proj[0], w_up[0], w_down[0], w_out)
    flags = decisions(slide[0] - 1, prev_states.shape[2])
    mods = modulation(timesteps[0], w_time, w_ada[0])
    opening = prev_states[0]
    field = opening.astype(BF16)

    for bit in reversed(range(bits)):
        other = swap(field, 1 << bit)
        if bit == bits - 2:
            weights = load(weights[:2]) + weights[2:]
        if bit == bits - 1:
            moved = swap(opening, 1)
            other, mods = together(other, mods)
        if bit == 0:
            field, opening, moved = together(field, opening, moved)
            opening = pick(flags, bits, opening, moved)
            moved = swap(opening, count // 2)
        field = pick(flags, bit, field, other)
    for sweep_index in range(SWEEPS):
        first = sweep_index == 0
        final = sweep_index == SWEEPS - 1
        halo, right, left = rim_of_neighbours(field)
        inc, weights = sweep(field, halo, right, left, mods, step_sizes, weights, first)
        if first:
            inc, opening, moved = together(inc, opening, moved)
            opening = pick(flags, 2 * bits - 1, opening, moved)
        before, total, sent = None, inc, inc.astype(BF16)
        for bit in range(bits - 1):
            other = swap(sent, 1 << bit)
            if first and bit + 1 < bits - 1:
                moved = swap(opening, 2 << bit)
                opening = pick(flags, bits + bit + 1, opening, moved)
            before, sent, total = add_block(
                flags, 2 * bits + bit, before, total, other, bit + 2 < bits
            )
        other = swap(sent, count // 2)
        field = add_last(
            flags, 3 * bits - 1, before, other, (opening, inc) if final else (opening,),
            F32 if final else BF16,
        )
    return field[None]


def solution(mesh):
    in_specs = (
        P(("groups", "win"), "gx", None), P(("groups", "win")), P(("groups", "win")),
        P(), P(), P(), P(), P(), P(), P(), P(), P(),
    )
    out_specs = P(("groups", "win"), "gx", None)
    return jax.shard_map(
        window_steps, mesh=mesh, in_specs=in_specs, out_specs=out_specs, check_vma=False
    )
```

```python
import functools
import math

import jax
import jax.numpy as jnp
from jax import lax
from jax.experimental import pallas as pl
from jax.experimental.pallas import tpu as pltpu
from jax.sharding import PartitionSpec as P

HEADS = 12
SWEEPS = 2
GY = 8
GZ = 8
REACH = 3
EPSILON = 1e-06
FAR = -(2.0**100)
LANES = 128
VMEM_LIMIT = 28 << 20
EMBED_PART = 128
QKV_TILE = 768
LEAD = 1
ATT_UNROLL = 4
PROJ_PART = 512
UP_TILE = 1536
DOWN_PART = 512
F32 = jnp.float32
BF16 = jnp.bfloat16


def dot(a, b):
    return lax.dot_general(a, b, (((1,), (0,)), ((), ())), preferred_element_type=F32)


def dot_t(a, b):
    return lax.dot_general(a, b, (((1,), (1,)), ((), ())), preferred_element_type=F32)


def layer_norm(values):
    centred = values - jnp.mean(values, axis=-1, keepdims=True)
    spread = jnp.mean(centred * centred, axis=-1, keepdims=True)
    return centred * lax.rsqrt(spread + EPSILON)


def silu(x):
    return x / (1.0 + jnp.exp(-x))


def gelu_of_half(half):
    rate = math.sqrt(2.0 / math.pi)
    inner = half * (2.0 * rate + (8.0 * rate * 0.044715) * (half * half))
    return half + half * jnp.tanh(inner)


def modulation_kernel(emb_ref, w_time_hbm, w_ada_hbm, mods_ref, w_time, w_ada, sems):
    parts, _, wide = w_ada.shape
    first = pltpu.make_async_copy(w_time_hbm, w_time, sems.at[0])
    first.start()
    blocks = []
    for i in range(parts):
        block = w_ada_hbm.at[:, pl.ds(i * wide, wide)]
        blocks.append(pltpu.make_async_copy(block, w_ada.at[i], sems.at[1 + i]))
        blocks[-1].start()
    first.wait()
    condition = silu(dot(emb_ref[...], w_time[...]))
    active = silu(condition).astype(BF16)
    for i in range(parts):
        blocks[i].wait()
        mods_ref[i] = dot(active, w_ada[i])


def in_hbm(x):
    return pltpu.with_memory_space_constraint(x, pltpu.HBM)


def load_kernel(*refs):
    count = len(refs) // 2
    sems = refs[-1]
    copies = [
        pltpu.make_async_copy(refs[i], refs[count + i], sems.at[i]) for i in range(count)
    ]
    for copy in copies:
        copy.start()
    for copy in copies:
        copy.wait()


def load(arrays):
    return tuple(
        pl.pallas_call(
            load_kernel,
            in_specs=[pl.BlockSpec(memory_space=pltpu.HBM)] * len(arrays),
            out_specs=[pl.BlockSpec(memory_space=pltpu.VMEM)] * len(arrays),
            out_shape=[pltpu.VMEM(x.shape, x.dtype) for x in arrays],
            scratch_shapes=[pltpu.SemaphoreType.DMA((len(arrays),))],
            compiler_params=pltpu.CompilerParams(vmem_limit_bytes=4 << 20),
            cost_estimate=pl.CostEstimate(
                flops=0, bytes_accessed=sum(2 * x.size for x in arrays), transcendentals=0
            ),
            name="load",
        )(*[in_hbm(x) for x in arrays])
    )


def modulation(moment, w_time, w_ada):
    half = w_time.shape[0] // 2
    freqs = jnp.exp(-math.log(10000.0) * jnp.arange(half, dtype=F32) / half)
    angles = moment.astype(F32) * freqs
    embedded = jnp.concatenate([jnp.cos(angles), jnp.sin(angles)]).astype(BF16)
    embedded = jnp.broadcast_to(embedded[None], (8, embedded.shape[0]))
    parts = 6
    depth, wide = w_ada.shape
    vmem = pl.BlockSpec(memory_space=pltpu.VMEM)
    hbm = pl.BlockSpec(memory_space=pltpu.HBM)
    return pl.pallas_call(
        modulation_kernel,
        in_specs=[vmem, hbm, hbm],
        out_specs=vmem,
        out_shape=jax.ShapeDtypeStruct((parts, 8, wide // parts), F32),
        scratch_shapes=[
            pltpu.VMEM(w_time.shape, w_time.dtype),
            pltpu.VMEM((parts, depth, wide // parts), w_ada.dtype),
            pltpu.SemaphoreType.DMA((1 + parts,)),
        ],
        compiler_params=pltpu.CompilerParams(vmem_limit_bytes=16 << 20),
        cost_estimate=pl.CostEstimate(
            flops=16 * w_ada.size, bytes_accessed=2 * w_ada.size, transcendentals=0
        ),
        name="modulation",
    )(embedded, in_hbm(w_time), in_hbm(w_ada))


def first_sweep_kernel(halo_right, halo_left, *refs):
    fields, ready, sources, (inc,), kept = refs[:4], refs[4:6], refs[6:10], refs[10:11], refs[11:15]
    scratch, sems = refs[15:-1], refs[-1]
    copies = [None] * len(ready)
    for i, (source, target) in enumerate(zip(sources, kept)):
        copies.append(pltpu.make_async_copy(source, target, sems.at[i]))
        copies[-1].start()
    sweep_kernel(halo_right, halo_left, *fields, *ready, *kept, inc, *scratch, arrived=copies)


def sweep_kernel(
    halo_right, halo_left,
    own_ref, halo_ref, mods_ref, step_ref,
    w_in, w_qkv, w_proj, w_up, w_down, w_out,
    inc_ref,
    h_scr, a_scr, b_scr, q_scr, k_scr, v_scr, o_scr, g_scr, qmask, kmask,
    arrived=None,
):
    def need(i):
        if arrived is not None and arrived[i] is not None:
            arrived[i].wait()

    rows, width = h_scr.shape
    rim = REACH * GY * GZ
    head = width // HEADS
    shift1, scale1 = mods_ref[0, 0:1, :], 1.0 + mods_ref[1, 0:1, :]
    shift2, scale2 = 0.5 * mods_ref[3, 0:1, :], 0.5 + 0.5 * mods_ref[4, 0:1, :]

    def place_of(shape):
        r = lax.broadcasted_iota(jnp.int32, shape, 0)
        f = lax.broadcasted_iota(jnp.int32, shape, 1)
        return f, r // (GY * GZ), (r // GZ) % GY, r % GZ

    f, plane, y, z = place_of(qmask.shape)
    hit = (f == y) | (f == GY + z) | (f == GY + GZ + plane)
    qmask[...] = jnp.where(hit, FAR, 0.0).astype(BF16)
    keys = kmask.shape[0]
    f, plane, y, z = place_of((GY * GZ, LANES))
    hit = (f == (y + GY // 2) % GY) | (f == GY + (z + GZ // 2) % GZ)
    near = jnp.where(hit, 1.0, 0.0).astype(BF16)
    end = jnp.where(f == GY + GZ, 1.0, 0.0).astype(BF16)
    start = jnp.where(f == GY + GZ + 1, 1.0, 0.0).astype(BF16)
    for p in range(2 * REACH + 2):
        more = {0: start, 2 * REACH + 1: end}.get(p)
        kmask[p * GY * GZ:(p + 1) * GY * GZ, :] = near if more is None else near + more

    need(0)

    def embed(x):
        h = dot(x, w_in[...])
        return h, (layer_norm(h) * scale1 + shift1).astype(BF16)

    a_scr[0:rim, :] = embed(halo_ref[halo_left:halo_left + rim, :])[1]
    a_scr[rim + rows:, :] = embed(halo_ref[halo_right:halo_right + rim, :])[1]
    for i in range(0, rows, EMBED_PART):
        h_scr[i:i + EMBED_PART, :], a_scr[rim + i:rim + i + EMBED_PART, :] = embed(
            own_ref[i:i + EMBED_PART, :]
        )

    need(1)
    unit = 1.0 / (math.sqrt(head) * math.log(2.0))

    @pl.loop(0, width // QKV_TILE)
    def _(j):
        at = pl.ds(pl.multiple_of(j * QKV_TILE, QKV_TILE), QKV_TILE)
        at_k = pl.ds(pl.multiple_of(width + j * QKV_TILE, QKV_TILE), QKV_TILE)
        at_v = pl.ds(pl.multiple_of(2 * width + j * QKV_TILE, QKV_TILE), QKV_TILE)
        q_scr[:, at] = (dot(a_scr[rim:rim + rows, :], w_qkv[:, at]) * unit).astype(BF16)
        k_scr[:, at] = dot(a_scr[...], w_qkv[:, at_k]).astype(BF16)
        v_scr[:, at] = dot(a_scr[...], w_qkv[:, at_v]).astype(BF16)

    lane = lax.broadcasted_iota(jnp.int32, (LANES, LANES), 1)
    first = lane < head

    @pl.loop(0, rows // LANES, unroll=ATT_UNROLL)
    def _(i):
        at = pl.ds(pl.multiple_of(i * LANES, LANES), LANES)
        window = pl.ds(pl.multiple_of(i * LANES, LANES), keys)
        qm = qmask[...]
        km = kmask[...]
        ones = jnp.ones((keys, LANES), BF16)
        zero = jnp.zeros((LANES, LANES), BF16)

        def scores(p):
            cols = slice(p * LANES, (p + 1) * LANES)
            q = q_scr[at, cols]
            qx = jnp.concatenate(
                [
                    jnp.concatenate([jnp.where(first, q, zero), qm], axis=1),
                    jnp.concatenate([jnp.where(first, zero, q), qm], axis=1),
                ],
                axis=0,
            )
            return dot_t(qx, jnp.concatenate([k_scr[window, cols], km], axis=1))

        def mix(p, s):
            cols = slice(p * LANES, (p + 1) * LANES)
            e = jnp.exp2(s - jnp.max(s, axis=-1, keepdims=True)).astype(BF16)
            o = dot(e, jnp.concatenate([v_scr[window, cols], ones], axis=1))
            num = jnp.where(first, o[:LANES, :LANES], o[LANES:, :LANES])
            den = jnp.where(first, o[:LANES, LANES:], o[LANES:, LANES:])
            o_scr[at, cols] = (num / den).astype(BF16)

        units = width // LANES
        waiting = [scores(p) for p in range(LEAD)]
        for p in range(units):
            if p + LEAD < units:
                waiting.append(scores(p + LEAD))
            mix(p, waiting.pop(0))

    need(2)
    for i in range(0, rows, PROJ_PART):
        at = slice(i, i + PROJ_PART)
        h = h_scr[at, :] + mods_ref[2, 0:1, :] * dot(o_scr[at, :], w_proj[...])
        h_scr[at, :] = h
        b_scr[at, :] = (layer_norm(h) * scale2 + shift2).astype(BF16)

    need(3)

    @pl.loop(0, w_up.shape[1] // UP_TILE)
    def _(j):
        at = pl.ds(pl.multiple_of(j * UP_TILE, UP_TILE), UP_TILE)
        g_scr[:, at] = gelu_of_half(dot(b_scr[...], w_up[:, at])).astype(BF16)

    need(4)
    need(5)
    step = step_ref[0]
    for i in range(0, rows, DOWN_PART):
        at = slice(i, i + DOWN_PART)
        h = h_scr[at, :] + mods_ref[5, 0:1, :] * dot(g_scr[at, :], w_down[...])
        out = step * dot(layer_norm(h).astype(BF16), w_out[...])
        inc_ref[at, :] = out


def sweep(own, halo, halo_right, halo_left, mods, step, weights, first):
    rows, channels = own.shape
    width, wide = weights[3].shape
    rim = REACH * GY * GZ
    full = rows + 2 * rim
    vmem = pl.BlockSpec(memory_space=pltpu.VMEM)
    hbm = pl.BlockSpec(memory_space=pltpu.HBM)
    scratch = [
        pltpu.VMEM((rows, width), F32),
        pltpu.VMEM((full, width), BF16),
        pltpu.VMEM((rows, width), BF16),
        pltpu.VMEM((rows, width), BF16),
        pltpu.VMEM((full, width), BF16),
        pltpu.VMEM((full, width), BF16),
        pltpu.VMEM((rows, width), BF16),
        pltpu.VMEM((rows, wide), BF16),
        pltpu.VMEM((LANES, LANES), BF16),
        pltpu.VMEM(((2 * REACH + 2) * GY * GZ, LANES), BF16),
    ]
    out_shape = [jax.ShapeDtypeStruct((rows, channels), F32)]
    kernel = sweep_kernel
    if first:
        kernel = first_sweep_kernel
        late = weights[2:]
        scratch.append(pltpu.SemaphoreType.DMA((len(late),)))
        out_shape += [pltpu.VMEM(w.shape, w.dtype) for w in late]
        weights = weights[:2] + tuple(in_hbm(w) for w in late)
    inc, *kept = pl.pallas_call(
        functools.partial(kernel, halo_right, halo_left),
        in_specs=[vmem, vmem, vmem, pl.BlockSpec(memory_space=pltpu.SMEM)]
        + [vmem] * 2
        + [hbm if first else vmem] * (len(weights) - 2),
        out_specs=[vmem] * len(out_shape),
        out_shape=out_shape,
        scratch_shapes=scratch,
        compiler_params=pltpu.CompilerParams(vmem_limit_bytes=VMEM_LIMIT),
        cost_estimate=pl.CostEstimate(
            flops=2 * rows * width * (4 * width + 2 * wide),
            bytes_accessed=sum(w.size * 2 for w in weights),
            transcendentals=0,
        ),
        name="first_sweep" if first else "sweep",
    )(own, halo, mods, step, *weights)
    return inc, weights[:2] + tuple(kept) if first else weights


def rim_of_neighbours(field):
    count = lax.axis_size("gx")
    rows = field.shape[0]
    rim = REACH * GY * GZ
    if count == 2:
        other = lax.ppermute(field, "gx", [(0, 1), (1, 0)])
        return other, 0, rows - rim
    right = lax.ppermute(field[:rim], "gx", [((i + 1) % count, i) for i in range(count)])
    left = lax.ppermute(field[-rim:], "gx", [(i, (i + 1) % count) for i in range(count)])
    return jnp.concatenate([right, left]), 0, rim


def swap(x, distance):
    count = lax.axis_size("win")
    return lax.ppermute(x, "win", [(i, i ^ distance) for i in range(count)])


def together(*values):
    return lax.optimization_barrier(values)


def small_call(kernel, args, out_shape):
    vmem = pl.BlockSpec(memory_space=pltpu.VMEM)
    return pl.pallas_call(
        kernel,
        in_specs=[vmem] * len(args),
        out_specs=jax.tree.map(lambda _: vmem, out_shape),
        out_shape=out_shape,
        compiler_params=pltpu.CompilerParams(vmem_limit_bytes=4 << 20),
    )(*args)


def decisions(offset, lanes):
    count = lax.axis_size("win")
    place = lax.axis_index("win")
    bit = jnp.arange(count.bit_length() - 1, dtype=jnp.int32)
    distance = jnp.left_shift(1, bit)
    low = place & (distance - 1)
    mine = jnp.right_shift(place, bit) & 1
    lands = jnp.right_shift(mine * distance + low - offset, bit) & 1
    last = count // distance - 1 - jnp.right_shift(offset, bit)
    clamped = (low == distance - 1) & (jnp.right_shift(place, bit) >= last)
    keep = jnp.where(clamped, mine == 1, lands == mine)
    near = (jnp.right_shift(place ^ offset, bit) & 1) == 0
    flags = jnp.concatenate([keep, near, mine == 1]).astype(jnp.int32)
    return jnp.broadcast_to(flags[:, None], (flags.shape[0], lanes))


def pick(flags, flag, own, other):
    def kernel(flags_ref, own_ref, other_ref, out_ref):
        own = flags_ref[flag:flag + 1, :] != 0
        out_ref[...] = jnp.where(own, own_ref[...], other_ref[...])

    return small_call(kernel, (flags, own, other), jax.ShapeDtypeStruct(own.shape, own.dtype))


def add_block(flags, flag, before, total, other, send, more):
    def kernel(flags_ref, *refs):
        refs = list(refs)
        start = refs.pop(0)[...] if before is not None else 0.0
        sums = refs.pop(0)[...]
        arrived = refs.pop(0)[...].astype(F32)
        above = flags_ref[flag:flag + 1, :] != 0
        refs.pop(0)[...] = start + jnp.where(above, arrived, 0.0)
        sums = sums + arrived
        for ref in refs:
            ref[...] = sums.astype(ref.dtype)

    wide = jax.ShapeDtypeStruct(total.shape, F32)
    narrow = jax.ShapeDtypeStruct(total.shape, BF16)
    args = (flags,) + (() if before is None else (before,)) + (total, other)
    outs = (wide,) + ((narrow,) if send else ()) + ((wide,) if more else ())
    out = small_call(kernel, args, outs)
    return out[0], out[1] if send else None, out[-1] if more else None


def offer(flags, bits, total, opening):
    def kernel(flags_ref, total_ref, opening_ref, out_ref):
        above = flags_ref[3 * bits - 1:3 * bits, :] != 0
        known = flags_ref[2 * bits - 1:2 * bits, :] != 0
        start = opening_ref[...]
        sums = total_ref[...] + jnp.where(known, start, 0.0)
        out_ref[...] = jnp.where(above, start, sums).astype(BF16)

    out = jax.ShapeDtypeStruct(total.shape, BF16)
    return small_call(kernel, (flags, total, opening), out)


def advance(flags, bits, before, other, opening):
    def kernel(flags_ref, before_ref, other_ref, opening_ref, out_ref):
        above = flags_ref[3 * bits - 1:3 * bits, :] != 0
        known = flags_ref[2 * bits - 1:2 * bits, :] != 0
        start = jnp.where(known, opening_ref[...], 0.0)
        wanted = above | jnp.logical_not(known)
        total = before_ref[...] + jnp.where(wanted, other_ref[...].astype(F32), 0.0)
        out_ref[...] = (start + total).astype(BF16)

    out = jax.ShapeDtypeStruct(before.shape, BF16)
    return small_call(kernel, (flags, before, other, opening), out)


def close(flags, flag, before, other, opening, inc):
    def kernel(flags_ref, before_ref, other_ref, opening_ref, inc_ref, out_ref):
        above = flags_ref[flag:flag + 1, :] != 0
        total = before_ref[...] + jnp.where(above, other_ref[...].astype(F32), 0.0)
        out_ref[...] = opening_ref[...] + (total + inc_ref[...])

    out = jax.ShapeDtypeStruct(inc.shape, F32)
    return small_call(kernel, (flags, before, other, opening, inc), out)


def window_steps(
    prev_states, timesteps, step_sizes, slide,
    w_time, w_ada, w_in, w_qkv, w_proj, w_up, w_down, w_out,
):
    count = lax.axis_size("win")
    bits = count.bit_length() - 1
    assert count == 1 << bits and bits > 1, "window size"
    weights = (w_in, w_qkv[0], w_proj[0], w_up[0], w_down[0], w_out)
    flags = decisions(slide[0] - 1, prev_states.shape[2])
    mods = modulation(timesteps[0], w_time, w_ada[0])
    opening = prev_states[0]
    field = opening.astype(BF16)

    inner = range(1, bits - 1)
    for bit in reversed(range(bits)):
        other = swap(field, 1 << bit)
        if bit == bits - 2:
            other, mods = together(other, mods)
        if bit == bits - 1:
            moved = swap(opening, 1)
            weights = load(weights[:2]) + weights[2:]
        if bit == 0:
            field, opening, moved = together(field, opening, moved)
            opening = pick(flags, bits, opening, moved)
            if inner:
                moved = swap(opening, 1 << inner[0])
        field = pick(flags, bit, field, other)
    for sweep_index in range(SWEEPS):
        first, final = sweep_index == 0, sweep_index == SWEEPS - 1
        halo, right, left = rim_of_neighbours(field)
        if final:
            field, opening = together(field, opening)
            moved = swap(opening, count // 2)
        inc, weights = sweep(field, halo, right, left, mods, step_sizes, weights, first)
        if first and inner:
            inc, opening, moved = together(inc, opening, moved)
            opening = pick(flags, bits + inner[0], opening, moved)
        if final:
            inc, opening, moved = together(inc, opening, moved)
            opening = pick(flags, 2 * bits - 1, opening, moved)
        before, total, sent = None, inc, inc.astype(BF16)
        for bit in range(bits - 1):
            other = swap(sent, 1 << bit)
            if first and bit + 2 in inner:
                moved = swap(opening, 4 << bit)
                opening = pick(flags, bits + bit + 2, opening, moved)
            before, sent, total = add_block(
                flags, 2 * bits + bit, before, total, other,
                send=bit + 2 < bits or final, more=bit + 2 < bits or not final,
            )
        if final:
            other = swap(sent, count // 2)
            field = close(flags, 3 * bits - 1, before, other, opening, inc)
        else:
            other = swap(offer(flags, bits, total, opening), count // 2)
            field = advance(flags, bits, before, other, opening)
    return field[None]


def solution(mesh):
    in_specs = (
        P(("groups", "win"), "gx", None), P(("groups", "win")), P(("groups", "win")),
        P(), P(), P(), P(), P(), P(), P(), P(), P(),
    )
    out_specs = P(("groups", "win"), "gx", None)
    return jax.shard_map(
        window_steps, mesh=mesh, in_specs=in_specs, out_specs=out_specs, check_vma=False
    )
```
